256 devices in a mesh: param: 16 (over x, y), space: 2 (over core), term: 8 (over z).
Axes of the slice: x: 4, y: 4, z: 8, core: 2. Of those that a mesh axis runs over, the one named last changes fastest.
Arguments:
- fields: float32 [128, 2, 8, 128, 128], P('param', None, None, 'space'), may hold values from -4 to 4
- library: int32 [168, 4], P('term'), may hold values from 0 to 6, as said below
- centers_x: int32 [16], replicated, may hold values from 0 to 127
- centers_y: int32 [16], replicated, may hold values from 0 to 127
- centers_t: int32 [4], replicated, may hold values from 0 to 7
- groups: int32 [168], replicated, may hold values from 0 to 23
Outputs:
- coefficients: float32 [128, 2, 168], P(('param', 'term'))
- misfit: float32 [128, 2, 168], P(('param', 'term'))
The draws below stay inside these ranges and needn't reach their ends.
Inputs may be any that keep to these rules, and one draw needn't show every extreme that they name: `library`: each row (a, b, dx, dy) gives powers a and b of 0 to 6 and derivative orders dx and dy of 0 to 2; rows are distinct, and a = b = 0 only with dx = dy = 0.
All inputs are finite; a program needn't handle non-finite values.
Results may differ from the reference program's by a relative error of at most 0.00011.
Values sent between devices are 32-bit elements; how exact they have to be, the bound alone decides.
A program may use at most 64 MiB of HBM per device.

```python
import jax
import jax.numpy as jnp
from jax import lax

NX = 128
NY = 128
NT = 8
POWERS = 7
TERMS = 168
KX = 16
KY = 16
KT = 4
TESTS = 1024
RX = 16
RT = 4
GROUPS = 24
PARAMS = 128


def draw_library(key, part):
    combos = POWERS * POWERS * 9 - 8
    chosen = jax.random.permutation(key, combos)[:TERMS].astype(jnp.int32)
    code_value = jnp.where(chosen == 0, 0, chosen + 8).astype(jnp.int32)
    return jnp.stack([code_value // (9 * POWERS), code_value // 9 % POWERS, code_value % 9 // 3, code_value % 3], axis=1).astype(jnp.int32)


def set_ends(values, stream_key, least, high):
    longest = values.shape.index(max(values.shape))
    spots = []
    for shift in (0, 1):
        where = [jax.random.randint(jax.random.fold_in(stream_key, axis), (), 0, length) for axis, length in enumerate(values.shape)]
        where[longest] = (where[longest] + shift) % values.shape[longest]
        spots.append(tuple(where))
    return values.at[spots[0]].set(least).at[spots[1]].set(high)


def levels(own_key, dims, split, smallest, top_value):
    loudness = 1.0
    for position, shards_of in split:
        heights = jax.random.uniform(jax.random.fold_in(jax.random.fold_in(own_key, 6), position), (shards_of,), jnp.float32, smallest / len(split), top_value / len(split))
        loudness = loudness * jnp.repeat(jnp.exp(heights), dims[position] // shards_of).reshape((-1,) + (1,) * (len(dims) - 1 - position))
    return loudness


def noise(own_key, dims, spread, reach, cuts=(), kind=jnp.bfloat16):
    factor_of = levels(own_key, dims, cuts, -0.22, 0.18) if cuts else 1.0
    result = jax.random.normal(own_key, dims, jnp.float32) * spread * factor_of
    return jnp.minimum(jnp.maximum(result, -reach), reach).astype(kind)


def setup_inputs(seed: int = 0) -> dict:
    keys = jax.random.split(jax.random.key(seed), 7)
    return {
        "fields": noise(keys[0], (PARAMS, 2, NT, NX, NY), 0.8, 4.0, ((0, 16), (3, 2)), jnp.float32),
        "library": draw_library(jax.random.fold_in(keys[6], 71), 0),
        "centers_x": set_ends(jax.random.randint(keys[2], (KX,), 0, NX), jax.random.fold_in(keys[2], 1), 0, NX - 1).astype(jnp.int32),
        "centers_y": set_ends(jax.random.randint(keys[3], (KY,), 0, NY), jax.random.fold_in(keys[3], 1), 0, NY - 1).astype(jnp.int32),
        "centers_t": set_ends(jax.random.randint(keys[4], (KT,), 0, NT), jax.random.fold_in(keys[4], 1), 0, NT - 1).astype(jnp.int32),
        "groups": set_ends(jax.random.randint(keys[5], (TERMS,), 0, GROUPS), jax.random.fold_in(keys[5], 1), 0, GROUPS - 1).astype(jnp.int32),
    }


highest = lax.Precision.HIGHEST

def space_table(centers, first_row, row_count, extent):
    cell_index = first_row + jnp.arange(row_count, dtype=jnp.int32)
    offset = (cell_index[None, :] - centers[:, None] + extent // 2) % extent - extent // 2
    scaled = offset.astype(jnp.float32) / RX
    bump_base = 1.0 - scaled * scaled
    inside = jnp.abs(scaled) < 1.0
    cube = bump_base * bump_base * bump_base
    bump_value = jnp.where(inside, cube * bump_base, 0.0)
    bump_first = jnp.where(inside, 8.0 * scaled * cube / RX, 0.0)
    bump_second = jnp.where(inside, -8.0 * (cube - 6.0 * scaled * scaled * bump_base * bump_base) / (RX * RX), 0.0)
    return jnp.stack([bump_value, bump_first, bump_second]).astype(jnp.float32)

def time_table(centers):
    step_index = jnp.arange(NT, dtype=jnp.int32)
    scaled = (step_index[None, :] - centers[:, None]).astype(jnp.float32) / RT
    bump_base = 1.0 - scaled * scaled
    inside = jnp.abs(scaled) < 1.0
    time_bump = jnp.where(inside, bump_base * bump_base, 0.0).astype(jnp.float32)
    time_slope = jnp.where(inside, 4.0 * scaled * bump_base / RT, 0.0).astype(jnp.float32)
    return (time_bump, time_slope)

def term_codes(library):
    return ((library[:, 0] * POWERS + library[:, 1]) * 9 + library[:, 2] * 3 + library[:, 3]).astype(jnp.int32)

def weak_rows(field_pair, x_table, y_table, time_bump, time_slope, term_code):
    species_u = field_pair[0]
    species_v = field_pair[1]
    powers_u = [jnp.ones_like(species_u)]
    powers_v = [jnp.ones_like(species_v)]
    for degree in range(1, POWERS):
        powers_u.append(powers_u[-1] * species_u)
        powers_v.append(powers_v[-1] * species_v)
    stack_u = jnp.stack(powers_u)
    stack_v = jnp.stack(powers_v)
    monomials = (stack_u[:, None] * stack_v[None, :]).reshape((POWERS * POWERS,) + species_u.shape)
    across_y = jnp.einsum('mtxy,dky->mtxdk', monomials, y_table, precision=highest)
    across_t = jnp.einsum('mtxdk,rt->mrxdk', across_y, time_bump, precision=highest)
    across_x = jnp.einsum('mrxdk,elx->medrkl', across_t, x_table, precision=highest)
    flat_table = across_x.reshape(POWERS * POWERS * 9, KT * KY * KX)
    features = jnp.take(flat_table, term_code, axis=0)
    source = across_y[jnp.array([POWERS, 1], dtype=jnp.int32)][:, :, :, 0, :]
    targets = jnp.einsum('stxk,rt,lx->srkl', source, time_slope, x_table[0], precision=highest)
    return jnp.concatenate([features, targets.reshape(2, KT * KY * KX)], axis=0)

def normalize(gram_matrix):
    diagonal = jnp.diagonal(gram_matrix, axis1=1, axis2=2)
    row_scale = jnp.sqrt(diagonal / TESTS + 1e-06)
    term_scale = row_scale[:, :TERMS]
    correlation = gram_matrix[:, :TERMS, :TERMS] / (TESTS * term_scale[:, :, None] * term_scale[:, None, :])
    right_side = gram_matrix[:, TERMS:, :TERMS] / (TESTS * term_scale[:, None, :] * row_scale[:, TERMS:, None])
    frobenius = jnp.sqrt(lax.optimization_barrier(jnp.sum(correlation * correlation, axis=(1, 2))))
    return (correlation, right_side, frobenius)

def group_squares(values, onehot):
    return jnp.dot(lax.optimization_barrier(jnp.sum(values * values, axis=(0, 1))), onehot, precision=highest)

def shrink(values, totals, onehot):
    threshold = 0.7 * jnp.sqrt(jnp.mean(totals))
    per_term = jnp.dot(onehot, totals, precision=highest)
    factor = jnp.maximum(0.0, 1.0 - threshold / jnp.sqrt(per_term + 1e-12))
    return values * factor

def correlate(correlation, values):
    return jnp.einsum('pij,psj->psi', correlation, values, precision=highest)

def reference(fields, library, centers_x, centers_y, centers_t, groups):
    x_table = space_table(centers_x, 0, NX, NX)
    y_table = space_table(centers_y, 0, NY, NY)
    time_bump, time_slope = time_table(centers_t)
    term_code = term_codes(library)

    def one_param(field_pair):
        integrals = weak_rows(field_pair, x_table, y_table, time_bump, time_slope, term_code)
        return jnp.dot(integrals, integrals.T, precision=highest)
    gram_matrix = lax.map(one_param, fields)
    correlation, right_side, frobenius = normalize(gram_matrix)
    onehot = (groups[:, None] == jnp.arange(GROUPS, dtype=jnp.int32)[None, :]).astype(jnp.float32)
    step_size = 1.0 / jnp.max(frobenius)
    first_guess = step_size * right_side
    first = shrink(first_guess, group_squares(first_guess, onehot), onehot)
    second_guess = first - step_size * (correlate(correlation, first) - right_side)
    second = shrink(second_guess, group_squares(second_guess, onehot), onehot)
    coefficients = second / step_size
    misfit = right_side - correlate(correlation, second)
    return (coefficients, misfit)
```

```python
import functools

import jax
import jax.numpy as jnp
from jax import lax
from jax.experimental import pallas as pl
from jax.experimental.pallas import tpu as pltpu
from jax.sharding import PartitionSpec as P

NX = 128
NY = 128
NT = 8
POWERS = 7
TERMS = 168
TESTS = 1024
GROUPS = 24
ROWS = 176
WIDE = 256
HALF = 64
GROUP_SIZE = 4
STEPS = 12
EARLY = 4

MESH = pl.DeviceIdType.MESH
f32 = jnp.float32
bf16 = jnp.bfloat16


def iota(shape, dim):
    return lax.broadcasted_iota(jnp.int32, shape, dim)


def split(value):
    high = value.astype(bf16)
    low = (value - high.astype(f32)).astype(bf16)
    return high, low


def bumps(offset):
    scaled = offset.astype(f32) / 16.0
    base = 1.0 - scaled * scaled
    inside = jnp.abs(scaled) < 1.0
    cube = base * base * base
    value = jnp.where(inside, cube * base, 0.0)
    first = jnp.where(inside, 8.0 * scaled * cube / 16.0, 0.0)
    second = jnp.where(inside, -8.0 * (cube - 6.0 * scaled * scaled * base * base) / 256.0, 0.0)
    return value, first, second


def pick_center(which, centers, count):
    total = jnp.zeros_like(which)
    for k in range(count):
        total = jnp.where(which == k, centers[k], total)
    return total


def dot(a, b):
    return jnp.dot(a, b, preferred_element_type=f32)


def dot_nt(a, b):
    return lax.dot_general(a, b, (((1,), (1,)), ((), ())), preferred_element_type=f32)


def kernel(
    n_param,
    n_term,
    fields,
    library,
    centers_x,
    centers_y,
    centers_t,
    groups,
    coefficients,
    misfit,
    pow_u,
    pow_v,
    m_hi,
    m_lo,
    w_hi,
    w_lo,
    bx_hi,
    bx_lo,
    table,
    rows_own,
    rows_far,
    a_hi,
    a_lo,
    corr,
    lib_all,
    code_v,
    code_s,
    msg,
    got_p,
    mid,
    got_t,
    field_sem,
    lib_send,
    lib_recv,
    code_sem,
    row_send,
    row_recv,
    p_send,
    p_recv,
    t_send,
    t_recv,
):
    me_p = lax.axis_index("param")
    me_s = lax.axis_index("space")
    me_t = lax.axis_index("term")
    local_terms = TERMS // n_term

    barrier = pltpu.get_barrier_semaphore()
    pl.semaphore_signal(barrier, inc=1, device_id={"space": 1 - me_s}, device_id_type=MESH)
    for d in range(1, n_param):
        peer = lax.rem(me_p + d, n_param)
        pl.semaphore_signal(barrier, inc=1, device_id={"param": peer}, device_id_type=MESH)
    for d in range(1, n_term):
        peer = lax.rem(me_t + d, n_term)
        pl.semaphore_signal(barrier, inc=1, device_id={"term": peer}, device_id_type=MESH)

    loads = []
    for s, powers in enumerate((pow_u, pow_v)):
        for t in range(NT):
            copy = pltpu.make_async_copy(
                fields.at[me_t, s, t],
                powers.at[1, :, pl.ds(t * NY, NY)],
                field_sem.at[s, t],
            )
            copy.start()
            loads.append(copy)

    lane = iota((NY, WIDE), 1)
    center = pick_center(lane & 15, centers_y, 16)
    offset = ((iota((NY, WIDE), 0) - center + 64) & 127) - 64
    value, first, second = bumps(offset)
    block = lane >> 6
    y_part = jnp.where(block == 1, first, jnp.where(block == 2, second, value))
    lane8 = iota((8, WIDE), 1)
    center_t = pick_center((lane8 >> 4) & 3, centers_t, 4)
    w_sum = jnp.zeros((1, WIDE), f32)
    y_sum = jnp.sum(y_part, axis=0, keepdims=True)
    for t in range(NT):
        scaled = (t - center_t).astype(f32) / 4.0
        base = 1.0 - scaled * scaled
        inside = jnp.abs(scaled) < 1.0
        bump = jnp.where(inside, base * base, 0.0)
        slope = jnp.where(inside, 4.0 * scaled * base / 4.0, 0.0)
        time = jnp.where((lane8 >> 6) == 3, slope, bump)[0:1]
        high, low = split(y_part * time)
        w_hi[pl.ds(t * NY, NY), :] = high
        w_lo[pl.ds(t * NY, NY), :] = low
        w_sum = w_sum + y_sum * time

    row = iota((48, WIDE), 0)
    lane = iota((48, WIDE), 1)
    center = pick_center(row & 15, centers_x, 16)
    offset = (((lane & 63) + me_s * HALF - center + 64) & 127) - 64
    value, first, second = bumps(offset)
    order = row >> 4
    x_part = jnp.where(order == 1, first, jnp.where(order == 2, second, value))
    for i in range(GROUP_SIZE):
        high, low = split(jnp.where((lane >> 6) == i, x_part, 0.0))
        bx_hi[pl.ds(i * 48, 48), :] = high
        bx_lo[pl.ds(i * 48, 48), :] = low

    x_sum = jnp.sum(jnp.where((lane >> 6) == 0, x_part, 0.0), axis=1, keepdims=True)
    for i in range(3):
        constant = x_sum[i * 16 : (i + 1) * 16] * w_sum
        table[2 * i] = constant[:, :NY]
        table[2 * i + 1] = constant[:, NY:]

    for copy in loads:
        copy.wait()
    pow_u[0] = jnp.ones((HALF, NT * NY), f32)
    pow_v[0] = jnp.ones((HALF, NT * NY), f32)
    for degree in range(2, POWERS):
        pow_u[degree] = pow_u[degree - 1] * pow_u[1]
        pow_v[degree] = pow_v[degree - 1] * pow_v[1]

    def group_step(g, carry):
        for i in range(GROUP_SIZE):
            q = g * GROUP_SIZE + (i + 1)
            a = q // POWERS
            b = q - a * POWERS
            high, low = split(pow_u[a] * pow_v[b])
            m_hi[pl.ds(i * HALF, HALF), :] = high
            m_lo[pl.ds(i * HALF, HALF), :] = low
        hi = m_hi[...]
        across = dot(hi, w_hi[...]) + dot(m_lo[...], w_hi[...]) + dot(hi, w_lo[...])
        s_hi, s_lo = split(across)
        out = dot(bx_hi[...], s_hi) + dot(bx_lo[...], s_hi) + dot(bx_hi[...], s_lo)
        for i in range(GROUP_SIZE * 3):
            spot = (g * GROUP_SIZE + 1) * 6 + 2 * i
            table[spot] = out[i * 16 : (i + 1) * 16, :NY]
            table[spot + 1] = out[i * 16 : (i + 1) * 16, NY:]
        return carry

    lax.fori_loop(0, EARLY, group_step, 0)

    pl.semaphore_wait(barrier, n_param + n_term - 1)
    lib_all[me_t] = library[...]
    lib_copies = []
    for d in range(1, n_term):
        peer = lax.rem(me_t + d, n_term)
        copy = pltpu.make_async_remote_copy(
            src_ref=library,
            dst_ref=lib_all.at[me_t],
            send_sem=lib_send.at[d],
            recv_sem=lib_recv.at[me_t],
            device_id={"term": peer},
            device_id_type=MESH,
        )
        copy.start()
        lib_copies.append(copy)

    lax.fori_loop(EARLY, STEPS, group_step, 0)

    for d, copy in enumerate(lib_copies, 1):
        copy.wait_send()
        peer = lax.rem(me_t + d, n_term)
        pltpu.make_async_remote_copy(
            src_ref=library,
            dst_ref=lib_all.at[peer],
            send_sem=lib_send.at[d],
            recv_sem=lib_recv.at[peer],
            device_id={"term": peer},
            device_id_type=MESH,
        ).wait_recv()
    for z in range(n_term):
        part = lib_all[z]
        code = ((part[0:1] * POWERS + part[1:2]) * 3 + part[2:3]) * 4 + part[3:4]
        code_v[z : z + 1, 0:local_terms] = code
    copy = pltpu.make_async_copy(code_v, code_s, code_sem)
    copy.start()
    copy.wait()

    left = iota((8, NY), 1) < 64

    def pick(index, odd):
        both = table[index]
        low, high = both[0:8], both[8:16]
        even_row = jnp.where(left, low, pltpu.roll(high, 64, 1))
        odd_row = jnp.where(left, pltpu.roll(low, 64, 1), high)
        return jnp.where(odd == 1, odd_row, even_row)

    def row_copy(c, count):
        return pltpu.make_async_remote_copy(
            src_ref=rows_own.at[pl.ds(c * local_terms * 8, count * 8), :],
            dst_ref=rows_far.at[pl.ds(c * local_terms * 8, count * 8), :],
            send_sem=row_send.at[c],
            recv_sem=row_recv.at[c],
            device_id={"space": 1 - me_s},
            device_id_type=MESH,
        )

    for s, monomial in enumerate((POWERS, 1)):
        rows_own[pl.ds((TERMS + s) * 8, 8), :] = pick(monomial * 6 + 1, 1)
    rows_own[pl.ds((TERMS + 2) * 8, (ROWS - TERMS - 2) * 8), :] = jnp.zeros(
        ((ROWS - TERMS - 2) * 8, NY), f32
    )

    def pick_step(z, carry):
        for i in range(local_terms):
            code = code_s[z, i]
            spot = pl.multiple_of((z * local_terms + i) * 8, 8)
            rows_own[pl.ds(spot, 8), :] = pick(code >> 1, code & 1)
        return carry

    pick_step(0, 0)
    tail_copy = row_copy(n_term, ROWS - TERMS)
    tail_copy.start()
    for z in range(1, n_term):
        pick_step(z, 0)
        row_copy(z - 1, local_terms).start()
    row_copy(n_term - 1, local_terms).start()

    group_row = groups[...]
    lane_w = iota((ROWS, WIDE), 1)
    row_w = iota((ROWS, WIDE), 0)
    eye = lane_w == row_w
    term_mask = (lane_w < TERMS) & (row_w < TERMS)
    wide_groups = jnp.where(iota((1, WIDE), 1) < TERMS, group_row, -1)
    group_col = jnp.sum(jnp.where(eye, wide_groups, 0), axis=1, keepdims=True)
    group_col = jnp.where(iota((ROWS, 1), 0) < TERMS, group_col, -1)
    onehot = jnp.where(group_col == iota((ROWS, NY), 1), 1.0, 0.0)
    onehot_t = jnp.where(wide_groups == iota((32, WIDE), 0), 1.0, 0.0)
    eye_g = iota((32, NY), 0) == iota((32, NY), 1)

    a_hi[pl.ds(ROWS, WIDE - ROWS), :] = jnp.zeros((WIDE - ROWS, TESTS), bf16)
    a_lo[pl.ds(ROWS, WIDE - ROWS), :] = jnp.zeros((WIDE - ROWS, TESTS), bf16)
    for z in range(n_term):
        row_copy(z, local_terms).wait()
    tail_copy.wait()

    for s in range(8):
        own = rows_own[pl.ds(s, ROWS, stride=8), :]
        far = rows_far[pl.ds(s, ROWS, stride=8), :]
        high, low = split(own + far)
        a_hi[pl.ds(0, ROWS), pl.ds(s * NY, NY)] = high
        a_lo[pl.ds(0, ROWS), pl.ds(s * NY, NY)] = low
    lhs = a_hi[pl.ds(0, ROWS), :]
    gram = (
        dot_nt(lhs, a_hi[...])
        + dot_nt(lhs, a_lo[...])
        + dot_nt(a_lo[pl.ds(0, ROWS), :], a_hi[...])
    )

    diagonal = jnp.where(eye, gram, 0.0)
    scale_row = 1.0 / jnp.sqrt(jnp.sum(diagonal, axis=0, keepdims=True) / TESTS + 1e-06)
    scale_col = 1.0 / jnp.sqrt(jnp.sum(diagonal, axis=1, keepdims=True) / TESTS + 1e-06)
    normal = gram * (scale_col / TESTS) * scale_row
    correlation = jnp.where(term_mask, normal, 0.0)
    corr[...] = correlation
    frobenius_sq = jnp.sum(jnp.sum(correlation * correlation, axis=1, keepdims=True), axis=0, keepdims=True)
    lane_row = iota((1, WIDE), 1)
    right_rows = []
    right_cols = []
    for s in range(2):
        right_rows.append(jnp.where(lane_row < TERMS, normal[TERMS + s : TERMS + s + 1], 0.0))
        column = jnp.sum(jnp.where(lane_w == TERMS + s, normal, 0.0), axis=1, keepdims=True)
        right_cols.append(jnp.where(iota((ROWS, 1), 0) < TERMS, column, 0.0))

    lane_g = iota((1, NY), 1)

    def combine(stack):
        return jnp.where(
            lane_g < GROUPS, jnp.sum(stack, axis=0), jnp.max(stack, axis=0)
        )

    def exchange(use, axis, count, me, source, target, send_sem, recv_sem):
        target[use, me] = source[use]
        copies = []
        for d in range(1, count):
            peer = lax.rem(me + d, count)
            copy = pltpu.make_async_remote_copy(
                src_ref=source.at[use],
                dst_ref=target.at[use, me],
                send_sem=send_sem.at[use, d],
                recv_sem=recv_sem.at[use, me],
                device_id={axis: peer},
                device_id_type=MESH,
            )
            copy.start()
            copies.append(copy)
        for d in range(1, count):
            peer = lax.rem(me + d, count)
            pltpu.make_async_remote_copy(
                src_ref=source.at[use],
                dst_ref=target.at[use, peer],
                send_sem=send_sem.at[use, d],
                recv_sem=recv_sem.at[use, peer],
                device_id={axis: peer},
                device_id_type=MESH,
            ).wait_recv()
        return copies

    def all_reduce(use, message):
        msg[use] = message
        sent = exchange(use, "param", n_param, me_p, msg, got_p, p_send, p_recv)
        mid[use] = combine(got_p[use])
        sent += exchange(use, "term", n_term, me_t, mid, got_t, t_send, t_recv)
        total = combine(got_t[use])
        return total, sent

    def factors(totals):
        valid = jnp.where(lane_g < GROUPS, totals, 0.0)
        mean = jnp.sum(valid, axis=1, keepdims=True) / GROUPS
        threshold = 0.7 * jnp.sqrt(mean)
        factor = jnp.maximum(0.0, 1.0 - threshold / jnp.sqrt(valid + 1e-12))
        factor = jnp.where(lane_g < GROUPS, factor, 0.0)
        col = jnp.sum(onehot * factor, axis=1, keepdims=True)
        group_factor = jnp.sum(jnp.where(eye_g, factor, 0.0), axis=1, keepdims=True)
        row = jnp.sum(onehot_t * group_factor, axis=0, keepdims=True)
        return row, col

    squares = right_cols[0] * right_cols[0] + right_cols[1] * right_cols[1]
    first_sq = jnp.sum(onehot * squares, axis=0, keepdims=True)
    message = jnp.where(lane_g < GROUPS, first_sq, frobenius_sq)
    total, sent_first = all_reduce(0, message)
    largest_sq = jnp.max(jnp.where(lane_g < GROUPS, 0.0, total), axis=1, keepdims=True)
    largest = jnp.sqrt(largest_sq)
    step_size = 1.0 / largest
    factor_row, factor_col = factors(total * (step_size * step_size))
    matrix = corr[...]
    guess_cols = []
    squares = jnp.zeros((ROWS, 1), f32)
    for s in range(2):
        first_row = step_size * right_rows[s] * factor_row
        first_col = step_size * right_cols[s] * factor_col
        product = jnp.sum(matrix * first_row, axis=1, keepdims=True)
        guess = first_col - step_size * (product - right_cols[s])
        squares = squares + guess * guess
        guess_cols.append(guess)
    second_sq = jnp.sum(onehot * squares, axis=0, keepdims=True)
    total, sent_second = all_reduce(1, jnp.where(lane_g < GROUPS, second_sq, 0.0))
    factor_row, factor_col = factors(total)
    for s in range(2):
        guess_row = jnp.sum(jnp.where(eye, guess_cols[s], 0.0), axis=0, keepdims=True)
        coefficient = guess_row * factor_row * largest
        product = jnp.sum(matrix * (guess_cols[s] * factor_col), axis=0, keepdims=True)
        coefficients[0, s : s + 1, :] = coefficient[:, :TERMS]
        misfit[0, s : s + 1, :] = (right_rows[s] - product)[:, :TERMS]
    for copy in sent_first + sent_second:
        copy.wait_send()


def body(fields, library, centers_x, centers_y, centers_t, groups):
    n_param = lax.axis_size("param")
    n_term = lax.axis_size("term")
    local_terms = library.shape[0]
    vmem = pl.BlockSpec(memory_space=pltpu.VMEM)
    smem = pl.BlockSpec(memory_space=pltpu.SMEM)
    out = jax.ShapeDtypeStruct((1, 2, TERMS), f32)
    wide_groups = jnp.pad(groups, (0, WIDE - TERMS)).reshape(1, WIDE)
    dma = pltpu.SemaphoreType.DMA
    return pl.pallas_call(
        functools.partial(kernel, n_param, n_term),
        out_shape=(out, out),
        in_specs=[pl.BlockSpec(memory_space=pl.ANY), vmem, smem, smem, smem, vmem],
        out_specs=(vmem, vmem),
        scratch_shapes=[
            pltpu.VMEM((POWERS, HALF, NT * NY), f32),
            pltpu.VMEM((POWERS, HALF, NT * NY), f32),
            pltpu.VMEM((GROUP_SIZE * HALF, NT * NY), bf16),
            pltpu.VMEM((GROUP_SIZE * HALF, NT * NY), bf16),
            pltpu.VMEM((NT * NY, WIDE), bf16),
            pltpu.VMEM((NT * NY, WIDE), bf16),
            pltpu.VMEM((GROUP_SIZE * 48, WIDE), bf16),
            pltpu.VMEM((GROUP_SIZE * 48, WIDE), bf16),
            pltpu.VMEM((POWERS * POWERS * 6, 16, NY), f32),
            pltpu.VMEM((ROWS * 8, NY), f32),
            pltpu.VMEM((ROWS * 8, NY), f32),
            pltpu.VMEM((WIDE, TESTS), bf16),
            pltpu.VMEM((WIDE, TESTS), bf16),
            pltpu.VMEM((ROWS, WIDE), f32),
            pltpu.VMEM((n_term, 4, local_terms), jnp.int32),
            pltpu.VMEM((8, NY), jnp.int32),
            pltpu.SMEM((8, NY), jnp.int32),
            pltpu.VMEM((2, 1, NY), f32),
            pltpu.VMEM((2, n_param, 1, NY), f32),
            pltpu.VMEM((2, 1, NY), f32),
            pltpu.VMEM((2, n_term, 1, NY), f32),
            dma((2, NT)),
            dma((n_term,)),
            dma((n_term,)),
            dma,
            dma((n_term + 1,)),
            dma((n_term + 1,)),
            dma((2, n_param)),
            dma((2, n_param)),
            dma((2, n_term)),
            dma((2, n_term)),
        ],
        compiler_params=pltpu.CompilerParams(
            collective_id=0, has_side_effects=True, vmem_limit_bytes=48 * 1024 * 1024
        ),
    )(fields, library.T, centers_x, centers_y, centers_t, wide_groups)


def solution(mesh):
    return jax.shard_map(
        body,
        mesh=mesh,
        in_specs=(P("param", None, None, "space", None), P("term", None), P(), P(), P(), P()),
        out_specs=(P(("param", "term"), None, None), P(("param", "term"), None, None)),
        check_vma=False,
    )
```

```python
import functools

import jax
import jax.numpy as jnp
from jax import lax
from jax.experimental import pallas as pl
from jax.experimental.pallas import tpu as pltpu
from jax.sharding import PartitionSpec as P

NX = 128
NY = 128
NT = 8
POWERS = 7
TERMS = 168
TESTS = 1024
GROUPS = 24
ROWS = 176
WIDE = 256
HALF = 64
GROUP_SIZE = 4
STEPS = 12
EARLY = 4

MESH = pl.DeviceIdType.MESH
f32 = jnp.float32
bf16 = jnp.bfloat16


def iota(shape, dim):
    return lax.broadcasted_iota(jnp.int32, shape, dim)


def split(value):
    high = value.astype(bf16)
    low = (value - high.astype(f32)).astype(bf16)
    return high, low


def bumps(offset):
    scaled = offset.astype(f32) / 16.0
    base = 1.0 - scaled * scaled
    inside = jnp.abs(scaled) < 1.0
    cube = base * base * base
    value = jnp.where(inside, cube * base, 0.0)
    first = jnp.where(inside, 8.0 * scaled * cube / 16.0, 0.0)
    second = jnp.where(inside, -8.0 * (cube - 6.0 * scaled * scaled * base * base) / 256.0, 0.0)
    return value, first, second


def pick_center(which, centers, count):
    total = jnp.zeros_like(which)
    for k in range(count):
        total = jnp.where(which == k, centers[k], total)
    return total


def dot(a, b):
    return jnp.dot(a, b, preferred_element_type=f32)


def dot_nt(a, b):
    return lax.dot_general(a, b, (((1,), (1,)), ((), ())), preferred_element_type=f32)


def kernel(
    n_param,
    n_term,
    fields,
    library_in,
    centers_x_in,
    centers_y_in,
    centers_t_in,
    groups_in,
    outputs,
    library,
    centers_x,
    centers_y,
    centers_t,
    groups,
    small_sem,
    pow_u,
    pow_v,
    m_hi,
    m_lo,
    w_hi,
    w_lo,
    bx_hi,
    bx_lo,
    table,
    rows_own,
    rows_far,
    a_hi,
    a_lo,
    corr,
    lib_all,
    code_v,
    code_s,
    msg,
    got_p,
    mid,
    got_t,
    field_sem,
    lib_send,
    lib_recv,
    code_sem,
    row_send,
    row_recv,
    p_send,
    p_recv,
    t_send,
    t_recv,
):
    me_p = lax.axis_index("param")
    me_s = lax.axis_index("space")
    me_t = lax.axis_index("term")
    local_terms = TERMS // n_term

    barrier = pltpu.get_barrier_semaphore()
    pl.semaphore_signal(barrier, inc=1, device_id={"space": 1 - me_s}, device_id_type=MESH)
    for d in range(1, n_param):
        peer = lax.rem(me_p + d, n_param)
        pl.semaphore_signal(barrier, inc=1, device_id={"param": peer}, device_id_type=MESH)
    for d in range(1, n_term):
        peer = lax.rem(me_t + d, n_term)
        pl.semaphore_signal(barrier, inc=1, device_id={"term": peer}, device_id_type=MESH)

    smalls = []
    for i, (source, target) in enumerate(
        (
            (centers_y_in, centers_y),
            (centers_t_in, centers_t),
            (centers_x_in, centers_x),
            (library_in, library),
            (groups_in, groups),
        )
    ):
        copy = pltpu.make_async_copy(source, target, small_sem.at[i])
        copy.start()
        smalls.append(copy)
    loads = []
    for s, powers in enumerate((pow_u, pow_v)):
        for t in range(NT):
            copy = pltpu.make_async_copy(
                fields.at[me_t, s, t],
                powers.at[1, :, pl.ds(t * NY, NY)],
                field_sem.at[s, t],
            )
            copy.start()
            loads.append(copy)

    for copy in smalls:
        copy.wait()

    lane = iota((NY, WIDE), 1)
    center = pick_center(lane & 15, centers_y, 16)
    offset = ((iota((NY, WIDE), 0) - center + 64) & 127) - 64
    value, first, second = bumps(offset)
    block = lane >> 6
    y_part = jnp.where(block == 1, first, jnp.where(block == 2, second, value))
    lane8 = iota((8, WIDE), 1)
    center_t = pick_center((lane8 >> 4) & 3, centers_t, 4)
    w_sum = jnp.zeros((1, WIDE), f32)
    y_sum = jnp.sum(y_part, axis=0, keepdims=True)
    for t in range(NT):
        scaled = (t - center_t).astype(f32) / 4.0
        base = 1.0 - scaled * scaled
        inside = jnp.abs(scaled) < 1.0
        bump = jnp.where(inside, base * base, 0.0)
        slope = jnp.where(inside, 4.0 * scaled * base / 4.0, 0.0)
        time = jnp.where((lane8 >> 6) == 3, slope, bump)[0:1]
        high, low = split(y_part * time)
        w_hi[pl.ds(t * NY, NY), :] = high
        w_lo[pl.ds(t * NY, NY), :] = low
        w_sum = w_sum + y_sum * time

    row = iota((48, WIDE), 0)
    lane = iota((48, WIDE), 1)
    center = pick_center(row & 15, centers_x, 16)
    offset = (((lane & 63) + me_s * HALF - center + 64) & 127) - 64
    value, first, second = bumps(offset)
    order = row >> 4
    x_part = jnp.where(order == 1, first, jnp.where(order == 2, second, value))
    for i in range(GROUP_SIZE):
        high, low = split(jnp.where((lane >> 6) == i, x_part, 0.0))
        bx_hi[pl.ds(i * 48, 48), :] = high
        bx_lo[pl.ds(i * 48, 48), :] = low

    x_sum = jnp.sum(jnp.where((lane >> 6) == 0, x_part, 0.0), axis=1, keepdims=True)
    for i in range(3):
        constant = x_sum[i * 16 : (i + 1) * 16] * w_sum
        table[2 * i] = constant[:, :NY]
        table[2 * i + 1] = constant[:, NY:]

    for copy in loads:
        copy.wait()
    pow_u[0] = jnp.ones((HALF, NT * NY), f32)
    pow_v[0] = jnp.ones((HALF, NT * NY), f32)
    for degree in range(2, POWERS):
        pow_u[degree] = pow_u[degree - 1] * pow_u[1]
        pow_v[degree] = pow_v[degree - 1] * pow_v[1]

    def group_step(g, carry):
        for i in range(GROUP_SIZE):
            q = g * GROUP_SIZE + (i + 1)
            a = q // POWERS
            b = q - a * POWERS
            high, low = split(pow_u[a] * pow_v[b])
            m_hi[pl.ds(i * HALF, HALF), :] = high
            m_lo[pl.ds(i * HALF, HALF), :] = low
        hi = m_hi[...]
        across = dot(hi, w_hi[...]) + dot(m_lo[...], w_hi[...]) + dot(hi, w_lo[...])
        s_hi, s_lo = split(across)
        out = dot(bx_hi[...], s_hi) + dot(bx_lo[...], s_hi) + dot(bx_hi[...], s_lo)
        for i in range(GROUP_SIZE * 3):
            spot = (g * GROUP_SIZE + 1) * 6 + 2 * i
            table[spot] = out[i * 16 : (i + 1) * 16, :NY]
            table[spot + 1] = out[i * 16 : (i + 1) * 16, NY:]
        return carry

    lax.fori_loop(0, EARLY, group_step, 0)

    pl.semaphore_wait(barrier, n_param + n_term - 1)
    lib_all[me_t] = library[...]
    lib_copies = []
    for d in range(1, n_term):
        peer = lax.rem(me_t + d, n_term)
        copy = pltpu.make_async_remote_copy(
            src_ref=library,
            dst_ref=lib_all.at[me_t],
            send_sem=lib_send.at[d],
            recv_sem=lib_recv.at[me_t],
            device_id={"term": peer},
            device_id_type=MESH,
        )
        copy.start()
        lib_copies.append(copy)

    lax.fori_loop(EARLY, STEPS, group_step, 0)

    for d, copy in enumerate(lib_copies, 1):
        copy.wait_send()
        peer = lax.rem(me_t + d, n_term)
        pltpu.make_async_remote_copy(
            src_ref=library,
            dst_ref=lib_all.at[peer],
            send_sem=lib_send.at[d],
            recv_sem=lib_recv.at[peer],
            device_id={"term": peer},
            device_id_type=MESH,
        ).wait_recv()
    for z in range(n_term):
        part = lib_all[z]
        code = ((part[0:1] * POWERS + part[1:2]) * 3 + part[2:3]) * 4 + part[3:4]
        code_v[z : z + 1, 0:local_terms] = code
    copy = pltpu.make_async_copy(code_v, code_s, code_sem)
    copy.start()
    copy.wait()

    left = iota((8, NY), 1) < 64

    def pick(index, odd):
        both = table[index]
        low, high = both[0:8], both[8:16]
        even_row = jnp.where(left, low, pltpu.roll(high, 64, 1))
        odd_row = jnp.where(left, pltpu.roll(low, 64, 1), high)
        return jnp.where(odd == 1, odd_row, even_row)

    def row_copy(c, count):
        return pltpu.make_async_remote_copy(
            src_ref=rows_own.at[pl.ds(c * local_terms * 8, count * 8), :],
            dst_ref=rows_far.at[pl.ds(c * local_terms * 8, count * 8), :],
            send_sem=row_send.at[c],
            recv_sem=row_recv.at[c],
            device_id={"space": 1 - me_s},
            device_id_type=MESH,
        )

    for s, monomial in enumerate((POWERS, 1)):
        rows_own[pl.ds((TERMS + s) * 8, 8), :] = pick(monomial * 6 + 1, 1)
    rows_own[pl.ds((TERMS + 2) * 8, (ROWS - TERMS - 2) * 8), :] = jnp.zeros(
        ((ROWS - TERMS - 2) * 8, NY), f32
    )

    def pick_step(z, carry):
        for i in range(local_terms):
            code = code_s[z, i]
            spot = pl.multiple_of((z * local_terms + i) * 8, 8)
            rows_own[pl.ds(spot, 8), :] = pick(code >> 1, code & 1)
        return carry

    pick_step(0, 0)
    tail_copy = row_copy(n_term, ROWS - TERMS)
    tail_copy.start()
    for z in range(1, n_term):
        pick_step(z, 0)
        row_copy(z - 1, local_terms).start()
    row_copy(n_term - 1, local_terms).start()

    lane_w = iota((ROWS, WIDE), 1)
    row_w = iota((ROWS, WIDE), 0)
    eye = lane_w == row_w
    term_mask = (lane_w < TERMS) & (row_w < TERMS)
    wide_groups = jnp.concatenate(
        [groups[...], jnp.full((1, WIDE - TERMS), -1, jnp.int32)], axis=1
    )
    group_col = jnp.sum(jnp.where(eye, wide_groups, 0), axis=1, keepdims=True)
    group_col = jnp.where(iota((ROWS, 1), 0) < TERMS, group_col, -1)
    onehot = jnp.where(group_col == iota((ROWS, NY), 1), 1.0, 0.0)
    onehot_t = jnp.where(wide_groups == iota((32, WIDE), 0), 1.0, 0.0)
    eye_g = iota((32, NY), 0) == iota((32, NY), 1)

    a_hi[pl.ds(ROWS, WIDE - ROWS), :] = jnp.zeros((WIDE - ROWS, TESTS), bf16)
    a_lo[pl.ds(ROWS, WIDE - ROWS), :] = jnp.zeros((WIDE - ROWS, TESTS), bf16)
    for z in range(n_term):
        row_copy(z, local_terms).wait()
    tail_copy.wait()

    for s in range(8):
        own = rows_own[pl.ds(s, ROWS, stride=8), :]
        far = rows_far[pl.ds(s, ROWS, stride=8), :]
        high, low = split(own + far)
        a_hi[pl.ds(0, ROWS), pl.ds(s * NY, NY)] = high
        a_lo[pl.ds(0, ROWS), pl.ds(s * NY, NY)] = low
    lhs = a_hi[pl.ds(0, ROWS), :]
    gram = (
        dot_nt(lhs, a_hi[...])
        + dot_nt(lhs, a_lo[...])
        + dot_nt(a_lo[pl.ds(0, ROWS), :], a_hi[...])
    )

    diagonal = jnp.where(eye, gram, 0.0)
    scale_row = 1.0 / jnp.sqrt(jnp.sum(diagonal, axis=0, keepdims=True) / TESTS + 1e-06)
    scale_col = 1.0 / jnp.sqrt(jnp.sum(diagonal, axis=1, keepdims=True) / TESTS + 1e-06)
    normal = gram * (scale_col / TESTS) * scale_row
    correlation = jnp.where(term_mask, normal, 0.0)
    corr[...] = correlation
    frobenius_sq = jnp.sum(jnp.sum(correlation * correlation, axis=1, keepdims=True), axis=0, keepdims=True)
    lane_row = iota((1, WIDE), 1)
    right_rows = []
    right_cols = []
    for s in range(2):
        right_rows.append(jnp.where(lane_row < TERMS, normal[TERMS + s : TERMS + s + 1], 0.0))
        column = jnp.sum(jnp.where(lane_w == TERMS + s, normal, 0.0), axis=1, keepdims=True)
        right_cols.append(jnp.where(iota((ROWS, 1), 0) < TERMS, column, 0.0))

    lane_g = iota((1, NY), 1)

    def combine(stack):
        return jnp.where(
            lane_g < GROUPS, jnp.sum(stack, axis=0), jnp.max(stack, axis=0)
        )

    def exchange(use, axis, count, me, source, target, send_sem, recv_sem):
        target[use, me] = source[use]
        copies = []
        for d in range(1, count):
            peer = lax.rem(me + d, count)
            copy = pltpu.make_async_remote_copy(
                src_ref=source.at[use],
                dst_ref=target.at[use, me],
                send_sem=send_sem.at[use, d],
                recv_sem=recv_sem.at[use, me],
                device_id={axis: peer},
                device_id_type=MESH,
            )
            copy.start()
            copies.append(copy)
        for d in range(1, count):
            peer = lax.rem(me + d, count)
            pltpu.make_async_remote_copy(
                src_ref=source.at[use],
                dst_ref=target.at[use, peer],
                send_sem=send_sem.at[use, d],
                recv_sem=recv_sem.at[use, peer],
                device_id={axis: peer},
                device_id_type=MESH,
            ).wait_recv()
        return copies

    def all_reduce(use, message):
        msg[use] = message
        sent = exchange(use, "param", n_param, me_p, msg, got_p, p_send, p_recv)
        mid[use] = combine(got_p[use])
        sent += exchange(use, "term", n_term, me_t, mid, got_t, t_send, t_recv)
        total = combine(got_t[use])
        return total, sent

    def factors(totals):
        valid = jnp.where(lane_g < GROUPS, totals, 0.0)
        mean = jnp.sum(valid, axis=1, keepdims=True) / GROUPS
        threshold = 0.7 * jnp.sqrt(mean)
        factor = jnp.maximum(0.0, 1.0 - threshold / jnp.sqrt(valid + 1e-12))
        factor = jnp.where(lane_g < GROUPS, factor, 0.0)
        col = jnp.sum(onehot * factor, axis=1, keepdims=True)
        group_factor = jnp.sum(jnp.where(eye_g, factor, 0.0), axis=1, keepdims=True)
        row = jnp.sum(onehot_t * group_factor, axis=0, keepdims=True)
        return row, col

    squares = right_cols[0] * right_cols[0] + right_cols[1] * right_cols[1]
    first_sq = jnp.sum(onehot * squares, axis=0, keepdims=True)
    message = jnp.where(lane_g < GROUPS, first_sq, frobenius_sq)
    total, sent_first = all_reduce(0, message)
    largest_sq = jnp.max(jnp.where(lane_g < GROUPS, 0.0, total), axis=1, keepdims=True)
    largest = jnp.sqrt(largest_sq)
    step_size = 1.0 / largest
    factor_row, factor_col = factors(total * (step_size * step_size))
    matrix = corr[...]
    guess_cols = []
    squares = jnp.zeros((ROWS, 1), f32)
    for s in range(2):
        first_row = step_size * right_rows[s] * factor_row
        first_col = step_size * right_cols[s] * factor_col
        product = jnp.sum(matrix * first_row, axis=1, keepdims=True)
        guess = first_col - step_size * (product - right_cols[s])
        squares = squares + guess * guess
        guess_cols.append(guess)
    second_sq = jnp.sum(onehot * squares, axis=0, keepdims=True)
    total, sent_second = all_reduce(1, jnp.where(lane_g < GROUPS, second_sq, 0.0))
    factor_row, factor_col = factors(total)
    for s in range(2):
        guess_row = jnp.sum(jnp.where(eye, guess_cols[s], 0.0), axis=0, keepdims=True)
        coefficient = guess_row * factor_row * largest
        product = jnp.sum(matrix * (guess_cols[s] * factor_col), axis=0, keepdims=True)
        outputs[0, s : s + 1, :] = coefficient[:, :TERMS]
        outputs[1, s : s + 1, :] = (right_rows[s] - product)[:, :TERMS]
    for copy in sent_first + sent_second:
        copy.wait_send()


def body(fields, library, centers_x, centers_y, centers_t, groups):
    n_param = lax.axis_size("param")
    n_term = lax.axis_size("term")
    local_terms = library.shape[0]
    vmem = pl.BlockSpec(memory_space=pltpu.VMEM)
    hbm = pl.BlockSpec(memory_space=pltpu.HBM)
    dma = pltpu.SemaphoreType.DMA
    outputs = pl.pallas_call(
        functools.partial(kernel, n_param, n_term),
        out_shape=jax.ShapeDtypeStruct((2, 2, TERMS), f32),
        in_specs=[hbm] * 6,
        out_specs=vmem,
        scratch_shapes=[
            pltpu.VMEM((4, local_terms), jnp.int32),
            pltpu.SMEM(centers_x.shape, jnp.int32),
            pltpu.SMEM(centers_y.shape, jnp.int32),
            pltpu.SMEM(centers_t.shape, jnp.int32),
            pltpu.VMEM((1, TERMS), jnp.int32),
            dma((5,)),
            pltpu.VMEM((POWERS, HALF, NT * NY), f32),
            pltpu.VMEM((POWERS, HALF, NT * NY), f32),
            pltpu.VMEM((GROUP_SIZE * HALF, NT * NY), bf16),
            pltpu.VMEM((GROUP_SIZE * HALF, NT * NY), bf16),
            pltpu.VMEM((NT * NY, WIDE), bf16),
            pltpu.VMEM((NT * NY, WIDE), bf16),
            pltpu.VMEM((GROUP_SIZE * 48, WIDE), bf16),
            pltpu.VMEM((GROUP_SIZE * 48, WIDE), bf16),
            pltpu.VMEM((POWERS * POWERS * 6, 16, NY), f32),
            pltpu.VMEM((ROWS * 8, NY), f32),
            pltpu.VMEM((ROWS * 8, NY), f32),
            pltpu.VMEM((WIDE, TESTS), bf16),
            pltpu.VMEM((WIDE, TESTS), bf16),
            pltpu.VMEM((ROWS, WIDE), f32),
            pltpu.VMEM((n_term, 4, local_terms), jnp.int32),
            pltpu.VMEM((8, NY), jnp.int32),
            pltpu.SMEM((8, NY), jnp.int32),
            pltpu.VMEM((2, 1, NY), f32),
            pltpu.VMEM((2, n_param, 1, NY), f32),
            pltpu.VMEM((2, 1, NY), f32),
            pltpu.VMEM((2, n_term, 1, NY), f32),
            dma((2, NT)),
            dma((n_term,)),
            dma((n_term,)),
            dma,
            dma((n_term + 1,)),
            dma((n_term + 1,)),
            dma((2, n_param)),
            dma((2, n_param)),
            dma((2, n_term)),
            dma((2, n_term)),
        ],
        compiler_params=pltpu.CompilerParams(
            collective_id=0, has_side_effects=True, vmem_limit_bytes=67043328
        ),
    )(fields, library.T, centers_x, centers_y, centers_t, groups.reshape(1, TERMS))
    return outputs[0:1], outputs[1:2]


def solution(mesh):
    return jax.shard_map(
        body,
        mesh=mesh,
        in_specs=(P("param", None, None, "space", None), P("term", None), P(), P(), P(), P()),
        out_specs=(P(("param", "term"), None, None), P(("param", "term"), None, None)),
        check_vma=False,
    )
```

```python
import functools

import jax
import jax.numpy as jnp
from jax import lax
from jax.experimental import pallas as pl
from jax.experimental.pallas import tpu as pltpu
from jax.sharding import PartitionSpec as P

NX = 128
NY = 128
NT = 8
POWERS = 7
TERMS = 168
TESTS = 1024
GROUPS = 24
ROWS = 176
WIDE = 256
HALF = 64
GROUP_SIZE = 4
STEPS = 12
EARLY = 4

MESH = pl.DeviceIdType.MESH
f32 = jnp.float32
bf16 = jnp.bfloat16


def iota(shape, dim):
    return lax.broadcasted_iota(jnp.int32, shape, dim)


def split(value):
    high = value.astype(bf16)
    low = (value - high.astype(f32)).astype(bf16)
    return high, low


def bumps(offset):
    scaled = offset.astype(f32) / 16.0
    base = 1.0 - scaled * scaled
    inside = jnp.abs(scaled) < 1.0
    cube = base * base * base
    value = jnp.where(inside, cube * base, 0.0)
    first = jnp.where(inside, 8.0 * scaled * cube / 16.0, 0.0)
    second = jnp.where(inside, -8.0 * (cube - 6.0 * scaled * scaled * base * base) / 256.0, 0.0)
    return value, first, second


def pick_center(which, centers, count):
    total = jnp.zeros_like(which)
    for k in range(count):
        total = jnp.where(which == k, centers[k], total)
    return total


def dot(a, b):
    return jnp.dot(a, b, preferred_element_type=f32)


def dot_nt(a, b):
    return lax.dot_general(a, b, (((1,), (1,)), ((), ())), preferred_element_type=f32)


def kernel(
    n_param,
    n_term,
    fields,
    library_in,
    centers_x_in,
    centers_y_in,
    centers_t_in,
    groups_in,
    outputs,
    library,
    centers_x,
    centers_y,
    centers_t,
    groups,
    small_sem,
    pow_u,
    pow_v,
    blocks,
    w_hi,
    w_lo,
    bx,
    held_hi,
    held_lo,
    table,
    rows_own,
    rows_far,
    a_hi,
    a_lo,
    corr,
    lib_all,
    code_v,
    code_s,
    msg,
    got_p,
    mid,
    got_t,
    field_sem,
    lib_send,
    lib_recv,
    code_sem,
    row_send,
    row_recv,
    p_send,
    p_recv,
    t_send,
    t_recv,
):
    me_p = lax.axis_index("param")
    me_s = lax.axis_index("space")
    me_t = lax.axis_index("term")
    local_terms = TERMS // n_term

    barrier = pltpu.get_barrier_semaphore()
    pl.semaphore_signal(barrier, inc=1, device_id={"space": 1 - me_s}, device_id_type=MESH)
    for d in range(1, n_param):
        peer = lax.rem(me_p + d, n_param)
        pl.semaphore_signal(barrier, inc=1, device_id={"param": peer}, device_id_type=MESH)
    for d in range(1, n_term):
        peer = lax.rem(me_t + d, n_term)
        pl.semaphore_signal(barrier, inc=1, device_id={"term": peer}, device_id_type=MESH)

    smalls = []
    for i, (source, target) in enumerate(
        (
            (centers_y_in, centers_y),
            (centers_t_in, centers_t),
            (centers_x_in, centers_x),
            (library_in, library),
            (groups_in, groups),
        )
    ):
        copy = pltpu.make_async_copy(source, target, small_sem.at[i])
        copy.start()
        smalls.append(copy)
    loads = []
    for s, powers in enumerate((pow_u, pow_v)):
        for t in range(NT):
            copy = pltpu.make_async_copy(
                fields.at[me_t, s, t],
                powers.at[1, :, pl.ds(t * NY, NY)],
                field_sem.at[s, t],
            )
            copy.start()
            loads.append(copy)

    for copy in smalls:
        copy.wait()

    lane = iota((NY, WIDE), 1)
    center = pick_center(lane & 15, centers_y, 16)
    offset = ((iota((NY, WIDE), 0) - center + 64) & 127) - 64
    value, first, second = bumps(offset)
    block = lane >> 6
    y_part = jnp.where(block == 1, first, jnp.where(block == 2, second, value))
    lane8 = iota((8, WIDE), 1)
    center_t = pick_center((lane8 >> 4) & 3, centers_t, 4)
    w_sum = jnp.zeros((1, WIDE), f32)
    y_sum = jnp.sum(y_part, axis=0, keepdims=True)
    for t in range(NT):
        scaled = (t - center_t).astype(f32) / 4.0
        base = 1.0 - scaled * scaled
        inside = jnp.abs(scaled) < 1.0
        bump = jnp.where(inside, base * base, 0.0)
        slope = jnp.where(inside, 4.0 * scaled * base / 4.0, 0.0)
        time = jnp.where((lane8 >> 6) == 3, slope, bump)[0:1]
        high, low = split(y_part * time)
        w_hi[pl.ds(t * NY, NY), :] = high
        w_lo[pl.ds(t * NY, NY), :] = low
        w_sum = w_sum + y_sum * time

    row = iota((48, WIDE), 0)
    lane = iota((48, WIDE), 1)
    center = pick_center(row & 15, centers_x, 16)
    offset = (((lane & 63) + me_s * HALF - center + 64) & 127) - 64
    value, first, second = bumps(offset)
    order = row >> 4
    x_part = jnp.where(order == 1, first, jnp.where(order == 2, second, value))
    for i in range(GROUP_SIZE):
        high, low = split(jnp.where((lane >> 6) == i, x_part, 0.0))
        bx[pl.ds(i * 48, 48), :] = high
        bx[pl.ds((GROUP_SIZE + i) * 48, 48), :] = low

    for copy in loads:
        copy.wait()
    pow_u[0] = jnp.ones((HALF, NT * NY), f32)
    pow_v[0] = jnp.ones((HALF, NT * NY), f32)
    for degree in range(2, POWERS):
        pow_u[degree] = pow_u[degree - 1] * pow_u[1]
        pow_v[degree] = pow_v[degree - 1] * pow_v[1]

    rows, height = GROUP_SIZE * 48, GROUP_SIZE * HALF

    def finish(g):
        both = dot(bx[...], held_hi[...])
        out = both[:rows] + both[rows:] + dot(bx[pl.ds(0, rows), :], held_lo[...])
        for i in range(GROUP_SIZE * 3):
            spot = (g * GROUP_SIZE + GROUP_SIZE) * 6 + 2 * i
            table[spot] = out[i * 16 : (i + 1) * 16, :NY]
            table[spot + 1] = out[i * 16 : (i + 1) * 16, NY:]

    def group_step(g, carry):
        finish(g - 1)
        for i in range(GROUP_SIZE):
            q = g * GROUP_SIZE + (i + 1)
            a = q // POWERS
            b = q - a * POWERS
            high, low = split(pow_u[a] * pow_v[b])
            blocks[pl.ds(i * HALF, HALF), :] = high
            blocks[pl.ds(height + i * HALF, HALF), :] = low
        both = dot(blocks[...], w_hi[...])
        across = both[:height] + both[height:] + dot(blocks[pl.ds(0, height), :], w_lo[...])
        high, low = split(across)
        held_hi[...] = high
        held_lo[...] = low
        return carry

    held_hi[...] = jnp.zeros((height, WIDE), bf16)
    held_lo[...] = jnp.zeros((height, WIDE), bf16)
    lax.fori_loop(0, EARLY, group_step, 0)

    pl.semaphore_wait(barrier, n_param + n_term - 1)
    lib_all[me_t] = library[...]
    lib_copies = []
    for d in range(1, n_term):
        peer = lax.rem(me_t + d, n_term)
        copy = pltpu.make_async_remote_copy(
            src_ref=library,
            dst_ref=lib_all.at[me_t],
            send_sem=lib_send.at[d],
            recv_sem=lib_recv.at[me_t],
            device_id={"term": peer},
            device_id_type=MESH,
        )
        copy.start()
        lib_copies.append(copy)

    lax.fori_loop(EARLY, STEPS, group_step, 0)
    finish(STEPS - 1)

    x_sum = jnp.sum(jnp.where((lane >> 6) == 0, x_part, 0.0), axis=1, keepdims=True)
    for i in range(3):
        constant = x_sum[i * 16 : (i + 1) * 16] * w_sum
        table[18 + 2 * i] = constant[:, :NY]
        table[18 + 2 * i + 1] = constant[:, NY:]

    for d, copy in enumerate(lib_copies, 1):
        copy.wait_send()
        peer = lax.rem(me_t + d, n_term)
        pltpu.make_async_remote_copy(
            src_ref=library,
            dst_ref=lib_all.at[peer],
            send_sem=lib_send.at[d],
            recv_sem=lib_recv.at[peer],
            device_id={"term": peer},
            device_id_type=MESH,
        ).wait_recv()
    for z in range(n_term):
        part = lib_all[z]
        code = ((part[0:1] * POWERS + part[1:2]) * 3 + part[2:3]) * 4 + part[3:4]
        code_v[z : z + 1, 0:local_terms] = code
    copy = pltpu.make_async_copy(code_v, code_s, code_sem)
    copy.start()
    copy.wait()

    left = iota((8, NY), 1) < 64

    def pick(index, odd):
        both = table[index]
        low, high = both[0:8], both[8:16]
        even_row = jnp.where(left, low, pltpu.roll(high, 64, 1))
        odd_row = jnp.where(left, pltpu.roll(low, 64, 1), high)
        return jnp.where(odd == 1, odd_row, even_row)

    def row_copy(c, count):
        return pltpu.make_async_remote_copy(
            src_ref=rows_own.at[pl.ds(c * local_terms * 8, count * 8), :],
            dst_ref=rows_far.at[pl.ds(c * local_terms * 8, count * 8), :],
            send_sem=row_send.at[c],
            recv_sem=row_recv.at[c],
            device_id={"space": 1 - me_s},
            device_id_type=MESH,
        )

    for s, monomial in enumerate((POWERS, 1)):
        rows_own[pl.ds((TERMS + s) * 8, 8), :] = pick(monomial * 6 + 19, 1)
    rows_own[pl.ds((TERMS + 2) * 8, (ROWS - TERMS - 2) * 8), :] = jnp.zeros(
        ((ROWS - TERMS - 2) * 8, NY), f32
    )

    def pick_step(z, carry):
        for i in range(local_terms):
            code = code_s[z, i]
            spot = pl.multiple_of((z * local_terms + i) * 8, 8)
            rows_own[pl.ds(spot, 8), :] = pick((code >> 1) + 18, code & 1)
        return carry

    pick_step(0, 0)
    tail_copy = row_copy(n_term, ROWS - TERMS)
    tail_copy.start()
    for z in range(1, n_term):
        pick_step(z, 0)
        row_copy(z - 1, local_terms).start()
    row_copy(n_term - 1, local_terms).start()

    lane_w = iota((ROWS, WIDE), 1)
    row_w = iota((ROWS, WIDE), 0)
    eye = lane_w == row_w
    term_mask = (lane_w < TERMS) & (row_w < TERMS)
    wide_groups = jnp.concatenate(
        [groups[...], jnp.full((1, WIDE - TERMS), -1, jnp.int32)], axis=1
    )
    group_col = jnp.sum(jnp.where(eye, wide_groups, 0), axis=1, keepdims=True)
    group_col = jnp.where(iota((ROWS, 1), 0) < TERMS, group_col, -1)
    onehot = jnp.where(group_col == iota((ROWS, NY), 1), 1.0, 0.0)
    onehot_t = jnp.where(wide_groups == iota((32, WIDE), 0), 1.0, 0.0)
    eye_g = iota((32, NY), 0) == iota((32, NY), 1)

    a_hi[pl.ds(ROWS, WIDE - ROWS), :] = jnp.zeros((WIDE - ROWS, TESTS), bf16)
    a_lo[pl.ds(ROWS, WIDE - ROWS), :] = jnp.zeros((WIDE - ROWS, TESTS), bf16)
    for z in range(n_term):
        row_copy(z, local_terms).wait()
    tail_copy.wait()

    for s in range(8):
        own = rows_own[pl.ds(s, ROWS, stride=8), :]
        far = rows_far[pl.ds(s, ROWS, stride=8), :]
        high, low = split(own + far)
        a_hi[pl.ds(0, ROWS), pl.ds(s * NY, NY)] = high
        a_lo[pl.ds(0, ROWS), pl.ds(s * NY, NY)] = low
    lhs = a_hi[pl.ds(0, ROWS), :]
    gram = (
        dot_nt(lhs, a_hi[...])
        + dot_nt(lhs, a_lo[...])
        + dot_nt(a_lo[pl.ds(0, ROWS), :], a_hi[...])
    )

    diagonal = jnp.where(eye, gram, 0.0)
    scale_row = 1.0 / jnp.sqrt(jnp.sum(diagonal, axis=0, keepdims=True) / TESTS + 1e-06)
    scale_col = 1.0 / jnp.sqrt(jnp.sum(diagonal, axis=1, keepdims=True) / TESTS + 1e-06)
    normal = gram * (scale_col / TESTS) * scale_row
    correlation = jnp.where(term_mask, normal, 0.0)
    corr[...] = correlation
    frobenius_sq = jnp.sum(jnp.sum(correlation * correlation, axis=1, keepdims=True), axis=0, keepdims=True)
    lane_row = iota((1, WIDE), 1)
    right_rows = []
    right_cols = []
    for s in range(2):
        right_rows.append(jnp.where(lane_row < TERMS, normal[TERMS + s : TERMS + s + 1], 0.0))
        column = jnp.sum(jnp.where(lane_w == TERMS + s, normal, 0.0), axis=1, keepdims=True)
        right_cols.append(jnp.where(iota((ROWS, 1), 0) < TERMS, column, 0.0))

    lane_g = iota((1, NY), 1)

    def combine(stack):
        return jnp.where(
            lane_g < GROUPS, jnp.sum(stack, axis=0), jnp.max(stack, axis=0)
        )

    def exchange(use, axis, count, me, source, target, send_sem, recv_sem):
        target[use, me] = source[use]
        copies = []
        for d in range(1, count):
            peer = lax.rem(me + d, count)
            copy = pltpu.make_async_remote_copy(
                src_ref=source.at[use],
                dst_ref=target.at[use, me],
                send_sem=send_sem.at[use, d],
                recv_sem=recv_sem.at[use, me],
                device_id={axis: peer},
                device_id_type=MESH,
            )
            copy.start()
            copies.append(copy)
        for d in range(1, count):
            peer = lax.rem(me + d, count)
            pltpu.make_async_remote_copy(
                src_ref=source.at[use],
                dst_ref=target.at[use, peer],
                send_sem=send_sem.at[use, d],
                recv_sem=recv_sem.at[use, peer],
                device_id={axis: peer},
                device_id_type=MESH,
            ).wait_recv()
        return copies

    def all_reduce(use, message):
        msg[use] = message
        sent = exchange(use, "param", n_param, me_p, msg, got_p, p_send, p_recv)
        mid[use] = combine(got_p[use])
        sent += exchange(use, "term", n_term, me_t, mid, got_t, t_send, t_recv)
        total = combine(got_t[use])
        return total, sent

    def factors(totals):
        valid = jnp.where(lane_g < GROUPS, totals, 0.0)
        mean = jnp.sum(valid, axis=1, keepdims=True) / GROUPS
        threshold = 0.7 * jnp.sqrt(mean)
        factor = jnp.maximum(0.0, 1.0 - threshold / jnp.sqrt(valid + 1e-12))
        factor = jnp.where(lane_g < GROUPS, factor, 0.0)
        col = jnp.sum(onehot * factor, axis=1, keepdims=True)
        group_factor = jnp.sum(jnp.where(eye_g, factor, 0.0), axis=1, keepdims=True)
        row = jnp.sum(onehot_t * group_factor, axis=0, keepdims=True)
        return row, col

    squares = right_cols[0] * right_cols[0] + right_cols[1] * right_cols[1]
    first_sq = jnp.sum(onehot * squares, axis=0, keepdims=True)
    message = jnp.where(lane_g < GROUPS, first_sq, frobenius_sq)
    total, sent_first = all_reduce(0, message)
    largest_sq = jnp.max(jnp.where(lane_g < GROUPS, 0.0, total), axis=1, keepdims=True)
    largest = jnp.sqrt(largest_sq)
    step_size = 1.0 / largest
    factor_row, factor_col = factors(total * (step_size * step_size))
    matrix = corr[...]
    guess_cols = []
    squares = jnp.zeros((ROWS, 1), f32)
    for s in range(2):
        first_row = step_size * right_rows[s] * factor_row
        first_col = step_size * right_cols[s] * factor_col
        product = jnp.sum(matrix * first_row, axis=1, keepdims=True)
        guess = first_col - step_size * (product - right_cols[s])
        squares = squares + guess * guess
        guess_cols.append(guess)
    second_sq = jnp.sum(onehot * squares, axis=0, keepdims=True)
    total, sent_second = all_reduce(1, jnp.where(lane_g < GROUPS, second_sq, 0.0))
    factor_row, factor_col = factors(total)
    for s in range(2):
        guess_row = jnp.sum(jnp.where(eye, guess_cols[s], 0.0), axis=0, keepdims=True)
        coefficient = guess_row * factor_row * largest
        product = jnp.sum(matrix * (guess_cols[s] * factor_col), axis=0, keepdims=True)
        outputs[0, s : s + 1, :] = coefficient[:, :TERMS]
        outputs[1, s : s + 1, :] = (right_rows[s] - product)[:, :TERMS]
    for copy in sent_first + sent_second:
        copy.wait_send()


def body(fields, library, centers_x, centers_y, centers_t, groups):
    n_param = lax.axis_size("param")
    n_term = lax.axis_size("term")
    local_terms = library.shape[0]
    vmem = pl.BlockSpec(memory_space=pltpu.VMEM)
    hbm = pl.BlockSpec(memory_space=pltpu.HBM)
    dma = pltpu.SemaphoreType.DMA
    outputs = pl.pallas_call(
        functools.partial(kernel, n_param, n_term),
        out_shape=jax.ShapeDtypeStruct((2, 2, TERMS), f32),
        in_specs=[hbm] * 6,
        out_specs=vmem,
        scratch_shapes=[
            pltpu.VMEM((4, local_terms), jnp.int32),
            pltpu.SMEM(centers_x.shape, jnp.int32),
            pltpu.SMEM(centers_y.shape, jnp.int32),
            pltpu.SMEM(centers_t.shape, jnp.int32),
            pltpu.VMEM((1, TERMS), jnp.int32),
            dma((5,)),
            pltpu.VMEM((POWERS, HALF, NT * NY), f32),
            pltpu.VMEM((POWERS, HALF, NT * NY), f32),
            pltpu.VMEM((2 * GROUP_SIZE * HALF, NT * NY), bf16),
            pltpu.VMEM((NT * NY, WIDE), bf16),
            pltpu.VMEM((NT * NY, WIDE), bf16),
            pltpu.VMEM((2 * GROUP_SIZE * 48, WIDE), bf16),
            pltpu.VMEM((GROUP_SIZE * HALF, WIDE), bf16),
            pltpu.VMEM((GROUP_SIZE * HALF, WIDE), bf16),
            pltpu.VMEM(((POWERS * POWERS + 3) * 6, 16, NY), f32),
            pltpu.VMEM((ROWS * 8, NY), f32),
            pltpu.VMEM((ROWS * 8, NY), f32),
            pltpu.VMEM((WIDE, TESTS), bf16),
            pltpu.VMEM((WIDE, TESTS), bf16),
            pltpu.VMEM((ROWS, WIDE), f32),
            pltpu.VMEM((n_term, 4, local_terms), jnp.int32),
            pltpu.VMEM((8, NY), jnp.int32),
            pltpu.SMEM((8, NY), jnp.int32),
            pltpu.VMEM((2, 1, NY), f32),
            pltpu.VMEM((2, n_param, 1, NY), f32),
            pltpu.VMEM((2, 1, NY), f32),
            pltpu.VMEM((2, n_term, 1, NY), f32),
            dma((2, NT)),
            dma((n_term,)),
            dma((n_term,)),
            dma,
            dma((n_term + 1,)),
            dma((n_term + 1,)),
            dma((2, n_param)),
            dma((2, n_param)),
            dma((2, n_term)),
            dma((2, n_term)),
        ],
        compiler_params=pltpu.CompilerParams(
            collective_id=0, has_side_effects=True, vmem_limit_bytes=67043328
        ),
    )(fields, library.T, centers_x, centers_y, centers_t, groups.reshape(1, TERMS))
    return outputs[0:1], outputs[1:2]


def solution(mesh):
    return jax.shard_map(
        body,
        mesh=mesh,
        in_specs=(P("param", None, None, "space", None), P("term", None), P(), P(), P(), P()),
        out_specs=(P(("param", "term"), None, None), P(("param", "term"), None, None)),
        check_vma=False,
    )
```

```python
import functools

import jax
import jax.numpy as jnp
from jax import lax
from jax.experimental import pallas as pl
from jax.experimental.pallas import tpu as pltpu
from jax.sharding import PartitionSpec as P

NX = 128
NY = 128
NT = 8
POWERS = 7
TERMS = 168
TESTS = 1024
GROUPS = 24
ROWS = 176
WIDE = 256
HALF = 64
GROUP_SIZE = 4
STEPS = 12
EARLY = 4
CHUNK = 128

MESH = pl.DeviceIdType.MESH
f32 = jnp.float32
bf16 = jnp.bfloat16


def iota(shape, dim):
    return lax.broadcasted_iota(jnp.int32, shape, dim)


def split(value):
    high = value.astype(bf16)
    low = (value - high.astype(f32)).astype(bf16)
    return high, low


def bumps(offset):
    scaled = offset.astype(f32) / 16.0
    base = 1.0 - scaled * scaled
    inside = jnp.abs(scaled) < 1.0
    cube = base * base * base
    value = jnp.where(inside, cube * base, 0.0)
    first = jnp.where(inside, 8.0 * scaled * cube / 16.0, 0.0)
    second = jnp.where(inside, -8.0 * (cube - 6.0 * scaled * scaled * base * base) / 256.0, 0.0)
    return value, first, second


def pick_center(which, centers, count):
    total = jnp.zeros_like(which)
    for k in range(count):
        total = jnp.where(which == k, centers[k], total)
    return total


def dot(a, b):
    return jnp.dot(a, b, preferred_element_type=f32)


def dot_nt(a, b):
    return lax.dot_general(a, b, (((1,), (1,)), ((), ())), preferred_element_type=f32)


def kernel(
    n_param,
    n_term,
    fields,
    library_in,
    centers_x_in,
    centers_y_in,
    centers_t_in,
    groups_in,
    outputs,
    library,
    centers_x,
    centers_y,
    centers_t,
    groups,
    small_sem,
    pow_u,
    pow_v,
    blocks,
    w_hi,
    w_lo,
    bx,
    held_hi,
    held_lo,
    table,
    rows_own,
    rows_far,
    a_hi,
    a_lo,
    corr,
    lib_all,
    code_v,
    code_s,
    msg,
    got_p,
    mid,
    got_t,
    field_sem,
    lib_send,
    lib_recv,
    code_sem,
    row_send,
    row_recv,
    p_send,
    p_recv,
    t_send,
    t_recv,
):
    me_p = lax.axis_index("param")
    me_s = lax.axis_index("space")
    me_t = lax.axis_index("term")
    local_terms = TERMS // n_term

    barrier = pltpu.get_barrier_semaphore()
    pl.semaphore_signal(barrier, inc=1, device_id={"space": 1 - me_s}, device_id_type=MESH)
    for d in range(1, n_param):
        peer = lax.rem(me_p + d, n_param)
        pl.semaphore_signal(barrier, inc=1, device_id={"param": peer}, device_id_type=MESH)
    for d in range(1, n_term):
        peer = lax.rem(me_t + d, n_term)
        pl.semaphore_signal(barrier, inc=1, device_id={"term": peer}, device_id_type=MESH)

    smalls = []
    for i, (source, target) in enumerate(
        (
            (centers_y_in, centers_y),
            (centers_t_in, centers_t),
            (centers_x_in, centers_x),
            (library_in, library),
            (groups_in, groups),
        )
    ):
        copy = pltpu.make_async_copy(source, target, small_sem.at[i])
        copy.start()
        smalls.append(copy)
    loads = []
    for s, powers in enumerate((pow_u, pow_v)):
        for t in range(NT):
            copy = pltpu.make_async_copy(
                fields.at[me_t, s, t],
                powers.at[1, :, pl.ds(t * NY, NY)],
                field_sem.at[s, t],
            )
            copy.start()
            loads.append(copy)

    for copy in smalls:
        copy.wait()

    lane = iota((NY, WIDE), 1)
    center = pick_center(lane & 15, centers_y, 16)
    offset = ((iota((NY, WIDE), 0) - center + 64) & 127) - 64
    value, first, second = bumps(offset)
    block = lane >> 6
    y_part = jnp.where(block == 1, first, jnp.where(block == 2, second, value))
    lane8 = iota((8, WIDE), 1)
    center_t = pick_center((lane8 >> 4) & 3, centers_t, 4)
    w_sum = jnp.zeros((1, WIDE), f32)
    y_sum = jnp.sum(y_part, axis=0, keepdims=True)
    for t in range(NT):
        scaled = (t - center_t).astype(f32) / 4.0
        base = 1.0 - scaled * scaled
        inside = jnp.abs(scaled) < 1.0
        bump = jnp.where(inside, base * base, 0.0)
        slope = jnp.where(inside, 4.0 * scaled * base / 4.0, 0.0)
        time = jnp.where((lane8 >> 6) == 3, slope, bump)[0:1]
        high, low = split(y_part * time)
        w_hi[pl.ds(t * NY, NY), :] = high
        w_lo[pl.ds(t * NY, NY), :] = low
        w_sum = w_sum + y_sum * time

    row = iota((48, WIDE), 0)
    lane = iota((48, WIDE), 1)
    center = pick_center(row & 15, centers_x, 16)
    offset = (((lane & 63) + me_s * HALF - center + 64) & 127) - 64
    value, first, second = bumps(offset)
    order = row >> 4
    x_part = jnp.where(order == 1, first, jnp.where(order == 2, second, value))
    for i in range(GROUP_SIZE):
        high, low = split(jnp.where((lane >> 6) == i, x_part, 0.0))
        bx[pl.ds(i * 48, 48), :] = high
        bx[pl.ds((GROUP_SIZE + i) * 48, 48), :] = low

    for copy in loads:
        copy.wait()
    pow_u[0] = jnp.ones((HALF, NT * NY), f32)
    pow_v[0] = jnp.ones((HALF, NT * NY), f32)
    for degree in range(2, POWERS):
        pow_u[degree] = pow_u[degree - 1] * pow_u[1]
        pow_v[degree] = pow_v[degree - 1] * pow_v[1]

    rows, height = GROUP_SIZE * 48, GROUP_SIZE * HALF

    left = iota((8, NY), 1) < 64

    def spread(spot, block):
        for i in range(2):
            low, high = block[0:8, i * NY : (i + 1) * NY], block[8:16, i * NY : (i + 1) * NY]
            table[spot + 2 * i] = jnp.where(left, low, pltpu.roll(high, 64, 1))
            table[spot + 2 * i + 1] = jnp.where(left, pltpu.roll(low, 64, 1), high)

    def finish(g):
        both = dot(bx[...], held_hi[...])
        out = both[:rows] + both[rows:] + dot(bx[pl.ds(0, rows), :], held_lo[...])
        for i in range(GROUP_SIZE * 3):
            spread((g * GROUP_SIZE + GROUP_SIZE) * 12 + 4 * i, out[i * 16 : (i + 1) * 16])

    def group_step(g, carry):
        finish(g - 1)
        for i in range(GROUP_SIZE):
            q = g * GROUP_SIZE + (i + 1)
            a = q // POWERS
            b = q - a * POWERS
            for k in range(NT * NY // CHUNK):
                columns = pl.ds(k * CHUNK, CHUNK)
                high, low = split(pow_u[a, :, columns] * pow_v[b, :, columns])
                blocks[pl.ds(i * HALF, HALF), columns] = high
                blocks[pl.ds(height + i * HALF, HALF), columns] = low
        both = dot(blocks[...], w_hi[...])
        across = both[:height] + both[height:] + dot(blocks[pl.ds(0, height), :], w_lo[...])
        high, low = split(across)
        held_hi[...] = high
        held_lo[...] = low
        return carry

    held_hi[...] = jnp.zeros((height, WIDE), bf16)
    held_lo[...] = jnp.zeros((height, WIDE), bf16)
    lax.fori_loop(0, EARLY, group_step, 0)

    pl.semaphore_wait(barrier, n_param + n_term - 1)
    lib_all[me_t] = library[...]
    lib_copies = []
    for d in range(1, n_term):
        peer = lax.rem(me_t + d, n_term)
        copy = pltpu.make_async_remote_copy(
            src_ref=library,
            dst_ref=lib_all.at[me_t],
            send_sem=lib_send.at[d],
            recv_sem=lib_recv.at[me_t],
            device_id={"term": peer},
            device_id_type=MESH,
        )
        copy.start()
        lib_copies.append(copy)

    lax.fori_loop(EARLY, STEPS, group_step, 0)
    finish(STEPS - 1)

    x_sum = jnp.sum(jnp.where((lane >> 6) == 0, x_part, 0.0), axis=1, keepdims=True)
    for i in range(3):
        constant = x_sum[i * 16 : (i + 1) * 16] * w_sum
        spread(36 + 4 * i, constant)

    for d, copy in enumerate(lib_copies, 1):
        copy.wait_send()
        peer = lax.rem(me_t + d, n_term)
        pltpu.make_async_remote_copy(
            src_ref=library,
            dst_ref=lib_all.at[peer],
            send_sem=lib_send.at[d],
            recv_sem=lib_recv.at[peer],
            device_id={"term": peer},
            device_id_type=MESH,
        ).wait_recv()
    for z in range(n_term):
        part = lib_all[z]
        code = ((part[0:1] * POWERS + part[1:2]) * 3 + part[2:3]) * 4 + part[3:4]
        code_v[z : z + 1, 0:local_terms] = code
    copy = pltpu.make_async_copy(code_v, code_s, code_sem)
    copy.start()
    copy.wait()

    def row_copy(c, count):
        return pltpu.make_async_remote_copy(
            src_ref=rows_own.at[pl.ds(c * local_terms * 8, count * 8), :],
            dst_ref=rows_far.at[pl.ds(c * local_terms * 8, count * 8), :],
            send_sem=row_send.at[c],
            recv_sem=row_recv.at[c],
            device_id={"space": 1 - me_s},
            device_id_type=MESH,
        )

    for s, monomial in enumerate((POWERS, 1)):
        rows_own[pl.ds((TERMS + s) * 8, 8), :] = table[monomial * 12 + 39]
    rows_own[pl.ds((TERMS + 2) * 8, (ROWS - TERMS - 2) * 8), :] = jnp.zeros(
        ((ROWS - TERMS - 2) * 8, NY), f32
    )

    def pick_step(z, carry):
        for i in range(local_terms):
            code = code_s[z, i]
            spot = pl.multiple_of((z * local_terms + i) * 8, 8)
            rows_own[pl.ds(spot, 8), :] = table[code + 36]
        return carry

    pick_step(0, 0)
    tail_copy = row_copy(n_term, ROWS - TERMS)
    tail_copy.start()
    for z in range(1, n_term):
        pick_step(z, 0)
        row_copy(z - 1, local_terms).start()
    row_copy(n_term - 1, local_terms).start()

    lane_w = iota((ROWS, WIDE), 1)
    row_w = iota((ROWS, WIDE), 0)
    eye = lane_w == row_w
    term_mask = (lane_w < TERMS) & (row_w < TERMS)
    wide_groups = jnp.concatenate(
        [groups[...], jnp.full((1, WIDE - TERMS), -1, jnp.int32)], axis=1
    )
    group_col = jnp.sum(jnp.where(eye, wide_groups, 0), axis=1, keepdims=True)
    group_col = jnp.where(iota((ROWS, 1), 0) < TERMS, group_col, -1)
    onehot = jnp.where(group_col == iota((ROWS, NY), 1), 1.0, 0.0)
    onehot_t = jnp.where(wide_groups == iota((32, WIDE), 0), 1.0, 0.0)
    eye_g = iota((32, NY), 0) == iota((32, NY), 1)

    a_hi[pl.ds(ROWS, WIDE - ROWS), :] = jnp.zeros((WIDE - ROWS, TESTS), bf16)
    a_lo[pl.ds(ROWS, WIDE - ROWS), :] = jnp.zeros((WIDE - ROWS, TESTS), bf16)
    for z in range(n_term):
        row_copy(z, local_terms).wait()
    tail_copy.wait()

    for s in range(8):
        own = rows_own[pl.ds(s, ROWS, stride=8), :]
        far = rows_far[pl.ds(s, ROWS, stride=8), :]
        high, low = split(own + far)
        a_hi[pl.ds(0, ROWS), pl.ds(s * NY, NY)] = high
        a_lo[pl.ds(0, ROWS), pl.ds(s * NY, NY)] = low
    lhs = a_hi[pl.ds(0, ROWS), :]
    gram = (
        dot_nt(lhs, a_hi[...])
        + dot_nt(lhs, a_lo[...])
        + dot_nt(a_lo[pl.ds(0, ROWS), :], a_hi[...])
    )

    diagonal = jnp.where(eye, gram, 0.0)
    scale_row = 1.0 / jnp.sqrt(jnp.sum(diagonal, axis=0, keepdims=True) / TESTS + 1e-06)
    scale_col = 1.0 / jnp.sqrt(jnp.sum(diagonal, axis=1, keepdims=True) / TESTS + 1e-06)
    normal = gram * (scale_col / TESTS) * scale_row
    correlation = jnp.where(term_mask, normal, 0.0)
    corr[...] = correlation
    frobenius_sq = jnp.sum(jnp.sum(correlation * correlation, axis=1, keepdims=True), axis=0, keepdims=True)
    lane_row = iota((1, WIDE), 1)
    right_rows = []
    right_cols = []
    for s in range(2):
        right_rows.append(jnp.where(lane_row < TERMS, normal[TERMS + s : TERMS + s + 1], 0.0))
        column = jnp.sum(jnp.where(lane_w == TERMS + s, normal, 0.0), axis=1, keepdims=True)
        right_cols.append(jnp.where(iota((ROWS, 1), 0) < TERMS, column, 0.0))

    lane_g = iota((1, NY), 1)

    def combine(stack):
        return jnp.where(
            lane_g < GROUPS, jnp.sum(stack, axis=0), jnp.max(stack, axis=0)
        )

    def exchange(use, axis, count, me, source, target, send_sem, recv_sem):
        target[use, me] = source[use]
        copies = []
        for d in range(1, count):
            peer = lax.rem(me + d, count)
            copy = pltpu.make_async_remote_copy(
                src_ref=source.at[use],
                dst_ref=target.at[use, me],
                send_sem=send_sem.at[use, d],
                recv_sem=recv_sem.at[use, me],
                device_id={axis: peer},
                device_id_type=MESH,
            )
            copy.start()
            copies.append(copy)
        for d in range(1, count):
            peer = lax.rem(me + d, count)
            pltpu.make_async_remote_copy(
                src_ref=source.at[use],
                dst_ref=target.at[use, peer],
                send_sem=send_sem.at[use, d],
                recv_sem=recv_sem.at[use, peer],
                device_id={axis: peer},
                device_id_type=MESH,
            ).wait_recv()
        return copies

    def all_reduce(use, message):
        msg[use] = message
        sent = exchange(use, "param", n_param, me_p, msg, got_p, p_send, p_recv)
        mid[use] = combine(got_p[use])
        sent += exchange(use, "term", n_term, me_t, mid, got_t, t_send, t_recv)
        total = combine(got_t[use])
        return total, sent

    def factors(totals):
        valid = jnp.where(lane_g < GROUPS, totals, 0.0)
        mean = jnp.sum(valid, axis=1, keepdims=True) / GROUPS
        threshold = 0.7 * jnp.sqrt(mean)
        factor = jnp.maximum(0.0, 1.0 - threshold / jnp.sqrt(valid + 1e-12))
        factor = jnp.where(lane_g < GROUPS, factor, 0.0)
        col = jnp.sum(onehot * factor, axis=1, keepdims=True)
        group_factor = jnp.sum(jnp.where(eye_g, factor, 0.0), axis=1, keepdims=True)
        row = jnp.sum(onehot_t * group_factor, axis=0, keepdims=True)
        return row, col

    squares = right_cols[0] * right_cols[0] + right_cols[1] * right_cols[1]
    first_sq = jnp.sum(onehot * squares, axis=0, keepdims=True)
    message = jnp.where(lane_g < GROUPS, first_sq, frobenius_sq)
    total, sent_first = all_reduce(0, message)
    largest_sq = jnp.max(jnp.where(lane_g < GROUPS, 0.0, total), axis=1, keepdims=True)
    largest = jnp.sqrt(largest_sq)
    step_size = 1.0 / largest
    factor_row, factor_col = factors(total * (step_size * step_size))
    matrix = corr[...]
    guess_cols = []
    squares = jnp.zeros((ROWS, 1), f32)
    for s in range(2):
        first_row = step_size * right_rows[s] * factor_row
        first_col = step_size * right_cols[s] * factor_col
        product = jnp.sum(matrix * first_row, axis=1, keepdims=True)
        guess = first_col - step_size * (product - right_cols[s])
        squares = squares + guess * guess
        guess_cols.append(guess)
    second_sq = jnp.sum(onehot * squares, axis=0, keepdims=True)
    total, sent_second = all_reduce(1, jnp.where(lane_g < GROUPS, second_sq, 0.0))
    factor_row, factor_col = factors(total)
    for s in range(2):
        guess_row = jnp.sum(jnp.where(eye, guess_cols[s], 0.0), axis=0, keepdims=True)
        coefficient = guess_row * factor_row * largest
        product = jnp.sum(matrix * (guess_cols[s] * factor_col), axis=0, keepdims=True)
        outputs[0, s : s + 1, :] = coefficient[:, :TERMS]
        outputs[1, s : s + 1, :] = (right_rows[s] - product)[:, :TERMS]
    for copy in sent_first + sent_second:
        copy.wait_send()


def body(fields, library, centers_x, centers_y, centers_t, groups):
    n_param = lax.axis_size("param")
    n_term = lax.axis_size("term")
    local_terms = library.shape[0]
    vmem = pl.BlockSpec(memory_space=pltpu.VMEM)
    hbm = pl.BlockSpec(memory_space=pltpu.HBM)
    dma = pltpu.SemaphoreType.DMA
    outputs = pl.pallas_call(
        functools.partial(kernel, n_param, n_term),
        out_shape=jax.ShapeDtypeStruct((2, 2, TERMS), f32),
        in_specs=[hbm] * 6,
        out_specs=vmem,
        scratch_shapes=[
            pltpu.VMEM((4, local_terms), jnp.int32),
            pltpu.SMEM(centers_x.shape, jnp.int32),
            pltpu.SMEM(centers_y.shape, jnp.int32),
            pltpu.SMEM(centers_t.shape, jnp.int32),
            pltpu.VMEM((1, TERMS), jnp.int32),
            dma((5,)),
            pltpu.VMEM((POWERS, HALF, NT * NY), f32),
            pltpu.VMEM((POWERS, HALF, NT * NY), f32),
            pltpu.VMEM((2 * GROUP_SIZE * HALF, NT * NY), bf16),
            pltpu.VMEM((NT * NY, WIDE), bf16),
            pltpu.VMEM((NT * NY, WIDE), bf16),
            pltpu.VMEM((2 * GROUP_SIZE * 48, WIDE), bf16),
            pltpu.VMEM((GROUP_SIZE * HALF, WIDE), bf16),
            pltpu.VMEM((GROUP_SIZE * HALF, WIDE), bf16),
            pltpu.VMEM(((POWERS * POWERS + 3) * 12, 8, NY), f32),
            pltpu.VMEM((ROWS * 8, NY), f32),
            pltpu.VMEM((ROWS * 8, NY), f32),
            pltpu.VMEM((WIDE, TESTS), bf16),
            pltpu.VMEM((WIDE, TESTS), bf16),
            pltpu.VMEM((ROWS, WIDE), f32),
            pltpu.VMEM((n_term, 4, local_terms), jnp.int32),
            pltpu.VMEM((8, NY), jnp.int32),
            pltpu.SMEM((8, NY), jnp.int32),
            pltpu.VMEM((2, 1, NY), f32),
            pltpu.VMEM((2, n_param, 1, NY), f32),
            pltpu.VMEM((2, 1, NY), f32),
            pltpu.VMEM((2, n_term, 1, NY), f32),
            dma((2, NT)),
            dma((n_term,)),
            dma((n_term,)),
            dma,
            dma((n_term + 1,)),
            dma((n_term + 1,)),
            dma((2, n_param)),
            dma((2, n_param)),
            dma((2, n_term)),
            dma((2, n_term)),
        ],
        compiler_params=pltpu.CompilerParams(
            collective_id=0, has_side_effects=True, vmem_limit_bytes=67043328
        ),
    )(fields, library.T, centers_x, centers_y, centers_t, groups.reshape(1, TERMS))
    return outputs[0:1], outputs[1:2]


def solution(mesh):
    return jax.shard_map(
        body,
        mesh=mesh,
        in_specs=(P("param", None, None, "space", None), P("term", None), P(), P(), P(), P()),
        out_specs=(P(("param", "term"), None, None), P(("param", "term"), None, None)),
        check_vma=False,
    )
```

```python
import functools

import jax
import jax.numpy as jnp
from jax import lax
from jax.experimental import pallas as pl
from jax.experimental.pallas import tpu as pltpu
from jax.sharding import PartitionSpec as P

NX = 128
NY = 128
NT = 8
POWERS = 7
TERMS = 168
TESTS = 1024
GROUPS = 24
ROWS = 176
WIDE = 256
HALF = 64
GROUP_SIZE = 4
STEPS = 12
EARLY = 4
CHUNK = 128

MESH = pl.DeviceIdType.MESH
f32 = jnp.float32
bf16 = jnp.bfloat16


def iota(shape, dim):
    return lax.broadcasted_iota(jnp.int32, shape, dim)


def split(value):
    high = value.astype(bf16)
    low = (value - high.astype(f32)).astype(bf16)
    return high, low


def bumps(offset):
    scaled = offset.astype(f32) / 16.0
    base = 1.0 - scaled * scaled
    inside = jnp.abs(scaled) < 1.0
    cube = base * base * base
    value = jnp.where(inside, cube * base, 0.0)
    first = jnp.where(inside, 8.0 * scaled * cube / 16.0, 0.0)
    second = jnp.where(inside, -8.0 * (cube - 6.0 * scaled * scaled * base * base) / 256.0, 0.0)
    return value, first, second


def pick_center(which, centers, count):
    total = jnp.zeros_like(which)
    for k in range(count):
        total = jnp.where(which == k, centers[k], total)
    return total


def dot(a, b):
    return jnp.dot(a, b, preferred_element_type=f32)


def dot_nt(a, b):
    return lax.dot_general(a, b, (((1,), (1,)), ((), ())), preferred_element_type=f32)


def kernel(
    n_param,
    n_term,
    fields,
    library_in,
    centers_x_in,
    centers_y_in,
    centers_t_in,
    groups_in,
    outputs,
    library,
    centers_x,
    centers_y,
    centers_t,
    groups,
    small_sem,
    pow_u,
    pow_v,
    blocks,
    w_hi,
    w_lo,
    bx,
    held_hi,
    held_lo,
    table,
    rows_own,
    rows_far,
    a_hi,
    a_lo,
    corr,
    lib_all,
    code_v,
    code_s,
    msg,
    got_p,
    mid,
    got_t,
    field_sem,
    lib_send,
    lib_recv,
    code_sem,
    row_send,
    row_recv,
    p_send,
    p_recv,
    t_send,
    t_recv,
):
    me_p = lax.axis_index("param")
    me_s = lax.axis_index("space")
    me_t = lax.axis_index("term")
    local_terms = TERMS // n_term

    barrier = pltpu.get_barrier_semaphore()
    pl.semaphore_signal(barrier, inc=1, device_id={"space": 1 - me_s}, device_id_type=MESH)
    for d in range(1, n_param):
        peer = lax.rem(me_p + d, n_param)
        pl.semaphore_signal(barrier, inc=1, device_id={"param": peer}, device_id_type=MESH)
    for d in range(1, n_term):
        peer = lax.rem(me_t + d, n_term)
        pl.semaphore_signal(barrier, inc=1, device_id={"term": peer}, device_id_type=MESH)

    smalls = []
    for i, (source, target) in enumerate(
        (
            (centers_y_in, centers_y),
            (centers_t_in, centers_t),
            (centers_x_in, centers_x),
            (library_in, library),
            (groups_in, groups),
        )
    ):
        copy = pltpu.make_async_copy(source, target, small_sem.at[i])
        copy.start()
        smalls.append(copy)
    loads = []
    for s, powers in enumerate((pow_u, pow_v)):
        for t in range(NT):
            copy = pltpu.make_async_copy(
                fields.at[me_t, s, t],
                powers.at[1, :, pl.ds(t * NY, NY)],
                field_sem.at[s, t],
            )
            copy.start()
            loads.append(copy)

    for copy in smalls:
        copy.wait()

    lane = iota((NY, WIDE), 1)
    center = pick_center(iota((8, WIDE), 1) & 15, centers_y, 16)[0:1]
    offset = ((iota((NY, WIDE), 0) - center + 64) & 127) - 64
    value, first, second = bumps(offset)
    block = lane >> 6
    y_part = jnp.where(block == 1, first, jnp.where(block == 2, second, value))
    lane8 = iota((8, WIDE), 1)
    center_t = pick_center((lane8 >> 4) & 3, centers_t, 4)
    w_sum = jnp.zeros((1, WIDE), f32)
    y_sum = jnp.sum(y_part, axis=0, keepdims=True)
    for t in range(NT):
        scaled = (t - center_t).astype(f32) / 4.0
        base = 1.0 - scaled * scaled
        inside = jnp.abs(scaled) < 1.0
        bump = jnp.where(inside, base * base, 0.0)
        slope = jnp.where(inside, 4.0 * scaled * base / 4.0, 0.0)
        time = jnp.where((lane8 >> 6) == 3, slope, bump)[0:1]
        high, low = split(y_part * time)
        w_hi[pl.ds(t * NY, NY), :] = high
        w_lo[pl.ds(t * NY, NY), :] = low
        w_sum = w_sum + y_sum * time

    row = iota((48, WIDE), 0)
    lane = iota((48, WIDE), 1)
    center = pick_center(iota((48, NY), 0) & 15, centers_x, 16)[:, 0:1]
    offset = (((lane & 63) + me_s * HALF - center + 64) & 127) - 64
    value, first, second = bumps(offset)
    order = row >> 4
    x_part = jnp.where(order == 1, first, jnp.where(order == 2, second, value))
    for i in range(GROUP_SIZE):
        high, low = split(jnp.where((lane >> 6) == i, x_part, 0.0))
        bx[pl.ds(i * 48, 48), :] = high
        bx[pl.ds((GROUP_SIZE + i) * 48, 48), :] = low

    pow_u[0] = jnp.ones((HALF, NT * NY), f32)
    pow_v[0] = jnp.ones((HALF, NT * NY), f32)
    for copy in loads:
        copy.wait()
    for powers in (pow_u, pow_v):
        for k in range(NT * NY // CHUNK):
            columns = pl.ds(k * CHUNK, CHUNK)
            base = powers[1, :, columns]
            product = base
            for degree in range(2, POWERS):
                product = product * base
                powers[degree, :, columns] = product

    rows, height = GROUP_SIZE * 48, GROUP_SIZE * HALF

    left = iota((8, NY), 1) < 64

    def spread(spot, block):
        for i in range(2):
            low, high = block[0:8, i * NY : (i + 1) * NY], block[8:16, i * NY : (i + 1) * NY]
            table[spot + 2 * i] = jnp.where(left, low, pltpu.roll(high, 64, 1))
            table[spot + 2 * i + 1] = jnp.where(left, pltpu.roll(low, 64, 1), high)

    def finish(g):
        both = dot(bx[...], held_hi[...])
        out = both[:rows] + both[rows:] + dot(bx[pl.ds(0, rows), :], held_lo[...])
        for i in range(GROUP_SIZE * 3):
            spread((g * GROUP_SIZE + GROUP_SIZE) * 12 + 4 * i, out[i * 16 : (i + 1) * 16])

    def group_step(g, carry):
        finish(g - 1)
        for i in range(GROUP_SIZE):
            q = g * GROUP_SIZE + (i + 1)
            a = q // POWERS
            b = q - a * POWERS
            for k in range(NT * NY // CHUNK):
                columns = pl.ds(k * CHUNK, CHUNK)
                high, low = split(pow_u[a, :, columns] * pow_v[b, :, columns])
                blocks[pl.ds(i * HALF, HALF), columns] = high
                blocks[pl.ds(height + i * HALF, HALF), columns] = low
        both = dot(blocks[...], w_hi[...])
        across = both[:height] + both[height:] + dot(blocks[pl.ds(0, height), :], w_lo[...])
        high, low = split(across)
        held_hi[...] = high
        held_lo[...] = low
        return carry

    held_hi[...] = jnp.zeros((height, WIDE), bf16)
    held_lo[...] = jnp.zeros((height, WIDE), bf16)
    lax.fori_loop(0, EARLY, group_step, 0)

    pl.semaphore_wait(barrier, n_param + n_term - 1)
    lib_all[me_t] = library[...]
    lib_copies = []
    for d in range(1, n_term):
        peer = lax.rem(me_t + d, n_term)
        copy = pltpu.make_async_remote_copy(
            src_ref=library,
            dst_ref=lib_all.at[me_t],
            send_sem=lib_send.at[d],
            recv_sem=lib_recv.at[me_t],
            device_id={"term": peer},
            device_id_type=MESH,
        )
        copy.start()
        lib_copies.append(copy)

    lax.fori_loop(EARLY, STEPS, group_step, 0)
    finish(STEPS - 1)

    x_sum = jnp.sum(jnp.where((lane >> 6) == 0, x_part, 0.0), axis=1, keepdims=True)
    for i in range(3):
        constant = x_sum[i * 16 : (i + 1) * 16] * w_sum
        spread(36 + 4 * i, constant)

    for d, copy in enumerate(lib_copies, 1):
        copy.wait_send()
        peer = lax.rem(me_t + d, n_term)
        pltpu.make_async_remote_copy(
            src_ref=library,
            dst_ref=lib_all.at[peer],
            send_sem=lib_send.at[d],
            recv_sem=lib_recv.at[peer],
            device_id={"term": peer},
            device_id_type=MESH,
        ).wait_recv()
    for z in range(n_term):
        part = lib_all[z]
        code = ((part[0:1] * POWERS + part[1:2]) * 3 + part[2:3]) * 4 + part[3:4]
        code_v[z : z + 1, 0:local_terms] = code
    copy = pltpu.make_async_copy(code_v, code_s, code_sem)
    copy.start()
    copy.wait()

    def row_copy(c, count):
        return pltpu.make_async_remote_copy(
            src_ref=rows_own.at[pl.ds(c * local_terms * 8, count * 8), :],
            dst_ref=rows_far.at[pl.ds(c * local_terms * 8, count * 8), :],
            send_sem=row_send.at[c],
            recv_sem=row_recv.at[c],
            device_id={"space": 1 - me_s},
            device_id_type=MESH,
        )

    for s, monomial in enumerate((POWERS, 1)):
        rows_own[pl.ds((TERMS + s) * 8, 8), :] = table[monomial * 12 + 39]
    rows_own[pl.ds((TERMS + 2) * 8, (ROWS - TERMS - 2) * 8), :] = jnp.zeros(
        ((ROWS - TERMS - 2) * 8, NY), f32
    )

    def pick_step(z, carry):
        for i in range(local_terms):
            code = code_s[z, i]
            spot = pl.multiple_of((z * local_terms + i) * 8, 8)
            rows_own[pl.ds(spot, 8), :] = table[code + 36]
        return carry

    pick_step(0, 0)
    tail_copy = row_copy(n_term, ROWS - TERMS)
    tail_copy.start()
    for z in range(1, n_term):
        pick_step(z, 0)
        row_copy(z - 1, local_terms).start()
    row_copy(n_term - 1, local_terms).start()

    lane_w = iota((ROWS, WIDE), 1)
    row_w = iota((ROWS, WIDE), 0)
    eye = lane_w == row_w
    term_mask = (lane_w < TERMS) & (row_w < TERMS)
    wide_groups = jnp.concatenate(
        [groups[...], jnp.full((1, WIDE - TERMS), -1, jnp.int32)], axis=1
    )
    group_col = jnp.sum(jnp.where(eye, wide_groups, 0), axis=1, keepdims=True)
    group_col = jnp.where(iota((ROWS, 1), 0) < TERMS, group_col, -1)
    onehot = jnp.where(group_col == iota((ROWS, NY), 1), 1.0, 0.0)
    onehot_t = jnp.where(wide_groups == iota((32, WIDE), 0), 1.0, 0.0)
    eye_g = iota((32, NY), 0) == iota((32, NY), 1)

    a_hi[pl.ds(ROWS, WIDE - ROWS), :] = jnp.zeros((WIDE - ROWS, TESTS), bf16)
    a_lo[pl.ds(ROWS, WIDE - ROWS), :] = jnp.zeros((WIDE - ROWS, TESTS), bf16)
    for z in range(n_term):
        row_copy(z, local_terms).wait()
    tail_copy.wait()

    for s in range(8):
        own = rows_own[pl.ds(s, ROWS, stride=8), :]
        far = rows_far[pl.ds(s, ROWS, stride=8), :]
        high, low = split(own + far)
        a_hi[pl.ds(0, ROWS), pl.ds(s * NY, NY)] = high
        a_lo[pl.ds(0, ROWS), pl.ds(s * NY, NY)] = low
    lhs = a_hi[pl.ds(0, ROWS), :]
    gram = (
        dot_nt(lhs, a_hi[...])
        + dot_nt(lhs, a_lo[...])
        + dot_nt(a_lo[pl.ds(0, ROWS), :], a_hi[...])
    )

    diagonal = jnp.where(eye, gram, 0.0)
    scale_row = 1.0 / jnp.sqrt(jnp.sum(diagonal, axis=0, keepdims=True) / TESTS + 1e-06)
    scale_col = 1.0 / jnp.sqrt(jnp.sum(diagonal, axis=1, keepdims=True) / TESTS + 1e-06)
    normal = gram * (scale_col / TESTS) * scale_row
    correlation = jnp.where(term_mask, normal, 0.0)
    corr[...] = correlation
    frobenius_sq = jnp.sum(jnp.sum(correlation * correlation, axis=1, keepdims=True), axis=0, keepdims=True)
    lane_row = iota((1, WIDE), 1)
    right_rows = []
    right_cols = []
    for s in range(2):
        right_rows.append(jnp.where(lane_row < TERMS, normal[TERMS + s : TERMS + s + 1], 0.0))
        column = jnp.sum(jnp.where(lane_w == TERMS + s, normal, 0.0), axis=1, keepdims=True)
        right_cols.append(jnp.where(iota((ROWS, 1), 0) < TERMS, column, 0.0))

    lane_g = iota((1, NY), 1)

    def combine(stack):
        return jnp.where(
            lane_g < GROUPS, jnp.sum(stack, axis=0), jnp.max(stack, axis=0)
        )

    def exchange(use, axis, count, me, source, target, send_sem, recv_sem):
        target[use, me] = source[use]
        copies = []
        for d in range(1, count):
            peer = lax.rem(me + d, count)
            copy = pltpu.make_async_remote_copy(
                src_ref=source.at[use],
                dst_ref=target.at[use, me],
                send_sem=send_sem.at[use, d],
                recv_sem=recv_sem.at[use, me],
                device_id={axis: peer},
                device_id_type=MESH,
            )
            copy.start()
            copies.append(copy)
        for d in range(1, count):
            peer = lax.rem(me + d, count)
            pltpu.make_async_remote_copy(
                src_ref=source.at[use],
                dst_ref=target.at[use, peer],
                send_sem=send_sem.at[use, d],
                recv_sem=recv_sem.at[use, peer],
                device_id={axis: peer},
                device_id_type=MESH,
            ).wait_recv()
        return copies

    def all_reduce(use, message):
        msg[use] = message
        sent = exchange(use, "param", n_param, me_p, msg, got_p, p_send, p_recv)
        mid[use] = combine(got_p[use])
        sent += exchange(use, "term", n_term, me_t, mid, got_t, t_send, t_recv)
        total = combine(got_t[use])
        return total, sent

    def factors(totals):
        valid = jnp.where(lane_g < GROUPS, totals, 0.0)
        mean = jnp.sum(valid, axis=1, keepdims=True) / GROUPS
        threshold = 0.7 * jnp.sqrt(mean)
        factor = jnp.maximum(0.0, 1.0 - threshold / jnp.sqrt(valid + 1e-12))
        factor = jnp.where(lane_g < GROUPS, factor, 0.0)
        col = jnp.sum(onehot * factor, axis=1, keepdims=True)
        group_factor = jnp.sum(jnp.where(eye_g, factor, 0.0), axis=1, keepdims=True)
        row = jnp.sum(onehot_t * group_factor, axis=0, keepdims=True)
        return row, col

    squares = right_cols[0] * right_cols[0] + right_cols[1] * right_cols[1]
    first_sq = jnp.sum(onehot * squares, axis=0, keepdims=True)
    message = jnp.where(lane_g < GROUPS, first_sq, frobenius_sq)
    total, sent_first = all_reduce(0, message)
    largest_sq = jnp.max(jnp.where(lane_g < GROUPS, 0.0, total), axis=1, keepdims=True)
    largest = jnp.sqrt(largest_sq)
    step_size = 1.0 / largest
    factor_row, factor_col = factors(total * (step_size * step_size))
    matrix = corr[...]
    guess_cols = []
    squares = jnp.zeros((ROWS, 1), f32)
    for s in range(2):
        first_row = step_size * right_rows[s] * factor_row
        first_col = step_size * right_cols[s] * factor_col
        product = jnp.sum(matrix * first_row, axis=1, keepdims=True)
        guess = first_col - step_size * (product - right_cols[s])
        squares = squares + guess * guess
        guess_cols.append(guess)
    second_sq = jnp.sum(onehot * squares, axis=0, keepdims=True)
    total, sent_second = all_reduce(1, jnp.where(lane_g < GROUPS, second_sq, 0.0))
    factor_row, factor_col = factors(total)
    for s in range(2):
        guess_row = jnp.sum(jnp.where(eye, guess_cols[s], 0.0), axis=0, keepdims=True)
        coefficient = guess_row * factor_row * largest
        product = jnp.sum(matrix * (guess_cols[s] * factor_col), axis=0, keepdims=True)
        outputs[0, s : s + 1, :] = coefficient[:, :TERMS]
        outputs[1, s : s + 1, :] = (right_rows[s] - product)[:, :TERMS]
    for copy in sent_first + sent_second:
        copy.wait_send()


def body(fields, library, centers_x, centers_y, centers_t, groups):
    n_param = lax.axis_size("param")
    n_term = lax.axis_size("term")
    local_terms = library.shape[0]
    vmem = pl.BlockSpec(memory_space=pltpu.VMEM)
    hbm = pl.BlockSpec(memory_space=pltpu.HBM)
    dma = pltpu.SemaphoreType.DMA
    outputs = pl.pallas_call(
        functools.partial(kernel, n_param, n_term),
        out_shape=jax.ShapeDtypeStruct((2, 2, TERMS), f32),
        in_specs=[hbm] * 6,
        out_specs=vmem,
        scratch_shapes=[
            pltpu.VMEM((4, local_terms), jnp.int32),
            pltpu.SMEM(centers_x.shape, jnp.int32),
            pltpu.SMEM(centers_y.shape, jnp.int32),
            pltpu.SMEM(centers_t.shape, jnp.int32),
            pltpu.VMEM((1, TERMS), jnp.int32),
            dma((5,)),
            pltpu.VMEM((POWERS, HALF, NT * NY), f32),
            pltpu.VMEM((POWERS, HALF, NT * NY), f32),
            pltpu.VMEM((2 * GROUP_SIZE * HALF, NT * NY), bf16),
            pltpu.VMEM((NT * NY, WIDE), bf16),
            pltpu.VMEM((NT * NY, WIDE), bf16),
            pltpu.VMEM((2 * GROUP_SIZE * 48, WIDE), bf16),
            pltpu.VMEM((GROUP_SIZE * HALF, WIDE), bf16),
            pltpu.VMEM((GROUP_SIZE * HALF, WIDE), bf16),
            pltpu.VMEM(((POWERS * POWERS + 3) * 12, 8, NY), f32),
            pltpu.VMEM((ROWS * 8, NY), f32),
            pltpu.VMEM((ROWS * 8, NY), f32),
            pltpu.VMEM((WIDE, TESTS), bf16),
            pltpu.VMEM((WIDE, TESTS), bf16),
            pltpu.VMEM((ROWS, WIDE), f32),
            pltpu.VMEM((n_term, 4, local_terms), jnp.int32),
            pltpu.VMEM((8, NY), jnp.int32),
            pltpu.SMEM((8, NY), jnp.int32),
            pltpu.VMEM((2, 1, NY), f32),
            pltpu.VMEM((2, n_param, 1, NY), f32),
            pltpu.VMEM((2, 1, NY), f32),
            pltpu.VMEM((2, n_term, 1, NY), f32),
            dma((2, NT)),
            dma((n_term,)),
            dma((n_term,)),
            dma,
            dma((n_term + 1,)),
            dma((n_term + 1,)),
            dma((2, n_param)),
            dma((2, n_param)),
            dma((2, n_term)),
            dma((2, n_term)),
        ],
        compiler_params=pltpu.CompilerParams(
            collective_id=0, has_side_effects=True, vmem_limit_bytes=67043328
        ),
    )(fields, library.T, centers_x, centers_y, centers_t, groups.reshape(1, TERMS))
    return outputs[0:1], outputs[1:2]


def solution(mesh):
    return jax.shard_map(
        body,
        mesh=mesh,
        in_specs=(P("param", None, None, "space", None), P("term", None), P(), P(), P(), P()),
        out_specs=(P(("param", "term"), None, None), P(("param", "term"), None, None)),
        check_vma=False,
    )
```
